768 devices in a mesh: frame: 96 (over x, z, core), head: 8 (over y).
Axes of the slice: x: 4, y: 8, z: 12, core: 2. Of those that a mesh axis runs over, the one named last changes fastest.
Arguments:
- queries: bfloat16 [49152, 3072], P('frame', 'head'), may hold values from -128 to 128
- keys: bfloat16 [49152, 3072], P('frame', 'head'), may hold values from -8 to 8
- values: bfloat16 [49152, 3072], P('frame', 'head'), may hold values from -6 to 6
- out_weight: bfloat16 [3072, 3072], P('head'), may hold values from -0.109375 to 0.109375
- span: int32 [96], replicated, may hold values from 1 to 8, as said below
- counts: int32 [96], replicated, may hold values from 128 to 512, as said below
Outputs:
- projected: bfloat16 [49152, 3072], P('frame', 'head')
The draws below stay inside these ranges and needn't reach their ends.
Inputs may be any that keep to these rules, and one draw needn't show every extreme that they name: `span`: every frame attends at least to itself; some frames reach the full window of 8 frames. `counts`: some frame is full and some frame holds exactly 128 live tokens.
All inputs are finite; a program needn't handle non-finite values.
Results may differ from the reference program's by a relative error of at most 0.02.
Values may be sent and summed in bfloat16 or wider, within the bound.
No kernel may reach another device: no remote copies, remote signals or barrier semaphores. Data moves between devices by JAX's collectives and lax.ppermute only.
A program may use at most 128 MiB of HBM per device.

```python
import jax
import jax.numpy as jnp
from jax import lax

D = 3072
HEADS = 24
HD = 128
WIN = 8
TOK = 512
FRAMES = 96
N_HEAD = 8


def base_keys(key):
    return jax.random.truncated_normal(jax.random.fold_in(key, 11), -6.0, 6.0, (FRAMES, TOK, HEADS, HD), jnp.float32)


def draw_keys(key, part):
    key_grid = base_keys(key)
    return key_grid.reshape(FRAMES * TOK, HEADS * HD).astype(jnp.bfloat16)


def draw_queries(key, part):
    gaussian = jax.random.truncated_normal(jax.random.fold_in(key, 12), -6.0, 6.0, (FRAMES, TOK, HEADS, HD), jnp.float32)
    return gaussian.reshape(FRAMES * TOK, HEADS * HD).astype(jnp.bfloat16)


def draw_span(key, part):
    frame_index = jnp.arange(FRAMES, dtype=jnp.int32)
    drawn = jax.random.randint(jax.random.fold_in(key, 21), (FRAMES,), 1, WIN + 1, jnp.int32)
    return jnp.where(frame_index % 5 == 0, WIN, drawn).astype(jnp.int32)


def draw_counts(key, part):
    frame_index = jnp.arange(FRAMES, dtype=jnp.int32)
    drawn = jax.random.randint(jax.random.fold_in(key, 22), (FRAMES,), TOK // 4, TOK + 1, jnp.int32)
    drawn = jnp.where(frame_index % 11 == 6, TOK // 4, drawn)
    return jnp.where(frame_index % 7 == 3, TOK, drawn).astype(jnp.int32)


def block_levels(rng, extent, shards, low, largest):
    level, own = 1.0, jax.random.fold_in(rng, 6)
    for dim, shards_of in shards:
        steps = jnp.exp(jax.random.uniform(jax.random.fold_in(own, dim), (shards_of,), jnp.float32, low / len(shards), largest / len(shards)))
        level = level * jnp.repeat(steps, extent[dim] // shards_of).reshape([-1 if axis == dim else 1 for axis in range(len(extent))])
    return level


def bell_draw(stream_key, shape, width, most, pieces=(), held_as=jnp.bfloat16):
    entries = width * jax.random.normal(stream_key, shape, jnp.float32)
    if pieces:
        entries = entries * block_levels(stream_key, shape, pieces, -0.22, 0.18)
    return jnp.clip(entries, -most, most).astype(held_as)


def setup_inputs(seed: int = 0) -> dict:
    arg_keys = jax.random.split(jax.random.key(seed), 7)
    return {
        "queries": draw_queries(jax.random.fold_in(arg_keys[6], 71), 0),
        "keys": draw_keys(jax.random.fold_in(arg_keys[6], 71), 0),
        "values": bell_draw(arg_keys[2], (FRAMES * TOK, HEADS * HD), 1.0, 6.0, ((0, 96), (1, 8))),
        "out_weight": bell_draw(arg_keys[3], (HEADS * HD, D), (HEADS * HD) ** -0.5, 0.109375, ((0, 8),)),
        "span": draw_span(jax.random.fold_in(arg_keys[6], 71), 0),
        "counts": draw_counts(jax.random.fold_in(arg_keys[6], 71), 0),
    }


def reference(queries, keys, values, out_weight, span, counts):
    scaling = HD ** -0.5
    query_grid = queries.reshape(FRAMES, TOK, HEADS, HD)
    padding = jnp.zeros(((WIN - 1) * TOK, HEADS * HD), jnp.bfloat16)
    key_padded = jnp.concatenate([padding, keys], axis=0).reshape(FRAMES + WIN - 1, TOK, HEADS, HD)
    value_padded = jnp.concatenate([padding, values], axis=0).reshape(FRAMES + WIN - 1, TOK, HEADS, HD)
    slot_index = jnp.arange(WIN * TOK, dtype=jnp.int32)

    def one_frame(own_frame):
        query_rows = query_grid[own_frame].astype(jnp.float32)
        key_rows = lax.dynamic_slice_in_dim(key_padded, own_frame, WIN, 0).reshape(WIN * TOK, HEADS, HD).astype(jnp.float32)
        value_rows = lax.dynamic_slice_in_dim(value_padded, own_frame, WIN, 0).reshape(WIN * TOK, HEADS, HD).astype(jnp.float32)
        sources = own_frame - (WIN - 1) + slot_index // TOK
        frame_counts = counts[jnp.clip(sources, 0, FRAMES - 1).astype(jnp.int32)]
        visible = (sources >= 0) & (own_frame - sources < span[own_frame]) & (slot_index % TOK < frame_counts)
        scores = jnp.einsum('thd,khd->htk', query_rows, key_rows) * scaling
        scores = jnp.where(visible[None, None, :], scores, -1e30)
        row_top = jnp.max(scores, axis=-1, keepdims=True)
        weights = jnp.exp(scores - row_top)
        row_total = jnp.sum(weights, axis=-1)
        rounded = lax.optimization_barrier(weights.astype(jnp.bfloat16)).astype(jnp.float32)
        mixed = jnp.einsum('htk,khd->thd', rounded, value_rows) / row_total.T[:, :, None]
        return mixed.reshape(TOK, HEADS * HD).astype(jnp.bfloat16)

    attention = lax.map(one_frame, jnp.arange(FRAMES, dtype=jnp.int32)).reshape(FRAMES * TOK, HEADS * HD)
    group_width = HEADS * HD // N_HEAD

    def add_group(group_index, summed):
        start = (group_index * group_width).astype(jnp.int32)
        columns = lax.dynamic_slice_in_dim(attention, start, group_width, 1)
        weight_rows = lax.dynamic_slice_in_dim(out_weight, start, group_width, 0)
        partial_value = jnp.dot(columns, weight_rows, preferred_element_type=jnp.float32)
        partial_value = lax.optimization_barrier(partial_value.astype(jnp.bfloat16)).astype(jnp.float32)
        return summed + partial_value

    summed = lax.fori_loop(0, N_HEAD, add_group, jnp.zeros((FRAMES * TOK, D), jnp.float32))
    return summed.astype(jnp.bfloat16)
```

```python
import jax
import jax.numpy as jnp
from jax import lax
from jax.experimental import pallas as pl
from jax.experimental.pallas import tpu as pltpu
from jax.sharding import PartitionSpec as P

HD = 128
WIN = 8
NEG = -1e30
EXP2_SCALE = HD ** (-0.5) * 1.4426950408889634
ROW_BLOCK = 256


def _attend(limit, q_ref, k_ref, v_ref, acc_ref, top_ref):
    slots = k_ref.shape[0]

    @pl.when(limit > 0)
    def _():
        keys = k_ref[...]
        values = jnp.concatenate([v_ref[...], jnp.ones((slots, HD), jnp.bfloat16)], axis=1)
        slot = lax.broadcasted_iota(jnp.int32, (1, slots), 1)
        hidden = jnp.where(slot < limit, 0.0, NEG)
        for start in range(0, q_ref.shape[0], ROW_BLOCK):
            rows = pl.ds(start, ROW_BLOCK)
            scores = lax.dot_general(
                q_ref[rows, :], keys, (((1,), (1,)), ((), ())), preferred_element_type=jnp.float32
            )
            scores = scores + hidden
            old_top = top_ref[0, rows, :]
            new_top = jnp.maximum(old_top, jnp.max(scores, axis=1, keepdims=True))
            wide_top = jnp.tile(new_top, (1, slots // HD))
            weights = jnp.exp2((scores - wide_top) * EXP2_SCALE).astype(jnp.bfloat16)
            rescale = jnp.exp2((old_top - new_top) * EXP2_SCALE)
            acc_ref[0, rows, :] = acc_ref[0, rows, :] * jnp.tile(rescale, (1, 2)) + jnp.dot(
                weights, values, preferred_element_type=jnp.float32
            )
            top_ref[0, rows, :] = new_top


def _visible(frame, side, behind, span_ref, counts_ref):
    query = frame if side == 0 else frame + 1 - 2 * (frame % 2)
    source = frame - behind
    back = query - source
    seen = (source >= 0) & (back >= 0) & (back < span_ref[query])
    return jnp.where(seen, counts_ref[jnp.maximum(source, 0)], 0)


def _start(acc, top):
    acc[...] = jnp.zeros_like(acc)
    top[...] = jnp.full_like(top, NEG)


def _attention_body(hops, first, hand_over):
    def body(frame_ref, span_ref, counts_ref, *refs):
        refs = list(refs)
        q_refs = [refs.pop(0), refs.pop(0)]
        kv_refs = [(refs.pop(0), refs.pop(0)) for _ in hops]
        if first:
            state_in = None
        else:
            state_in = [refs.pop(0) for _ in range(4)]
        if hand_over:
            own_acc, own_top, packed, other_acc, other_top = refs
        else:
            own_acc, own_top, other_acc, other_top = refs
        state = (own_acc, own_top, other_acc, other_top)
        if first:
            _start(own_acc, own_top)
            _start(other_acc, other_top)
        else:
            for ref, ref_in in zip(state, state_in):
                ref[...] = ref_in[...]
        frame = frame_ref[0]
        for hop, (k_ref, v_ref) in zip(hops, kv_refs):
            for side in (0, 1):
                limit = _visible(frame, side, 2 * hop, span_ref, counts_ref)
                _attend(limit, q_refs[side], k_ref, v_ref, state[2 * side], state[2 * side + 1])
        if hand_over:
            lane = lax.broadcasted_iota(jnp.int32, (1, HD), 1)
            packed[0, :, :HD] = other_acc[0, :, :HD]
            packed[0, :, HD:] = jnp.where(lane < HD // 2, other_top[0], other_acc[0, :, HD:])

    return body


def attention_call(scalars, q_own, q_other, sources, hops, state, head0, heads, hand_over, name):
    per_frame = q_own.shape[0]
    first = state is None
    q_spec = pl.BlockSpec((per_frame, HD), lambda h, *_: (0, head0 + h))
    k_spec = pl.BlockSpec((per_frame, HD), lambda h, *_: (0, h))
    v_spec = pl.BlockSpec((per_frame, HD), lambda h, *_: (0, heads + h))
    acc_spec = pl.BlockSpec((1, per_frame, 2 * HD), lambda h, *_: (h, 0, 0))
    top_spec = pl.BlockSpec((1, per_frame, HD), lambda h, *_: (h, 0, 0))
    in_specs = [q_spec, q_spec]
    operands = [q_own, q_other]
    for source in sources:
        in_specs += [k_spec, v_spec]
        operands += [source, source]
    if not first:
        in_specs += [acc_spec, top_spec] * 2
        operands += list(state)
    acc_shape = jax.ShapeDtypeStruct((heads, per_frame, 2 * HD), jnp.float32)
    top_shape = jax.ShapeDtypeStruct((heads, per_frame, HD), jnp.float32)
    scratch = []
    if hand_over:
        out_specs = [acc_spec, top_spec, acc_spec]
        out_shape = [acc_shape, top_shape, acc_shape]
        scratch = [
            pltpu.VMEM((1, per_frame, 2 * HD), jnp.float32),
            pltpu.VMEM((1, per_frame, HD), jnp.float32),
        ]
    else:
        out_specs = [acc_spec, top_spec] * 2
        out_shape = [acc_shape, top_shape] * 2
    pairs = 2 * len(hops) * heads * per_frame * per_frame
    return pl.pallas_call(
        _attention_body(hops, first, hand_over),
        out_shape=out_shape,
        grid_spec=pltpu.PrefetchScalarGridSpec(
            num_scalar_prefetch=3,
            grid=(heads,),
            in_specs=in_specs,
            out_specs=out_specs,
            scratch_shapes=scratch,
        ),
        cost_estimate=pl.CostEstimate(
            flops=pairs * HD * 8, transcendentals=pairs, bytes_accessed=per_frame * HD * 16 * heads
        ),
        compiler_params=pltpu.CompilerParams(vmem_limit_bytes=40 << 20),
        name=name,
    )(*scalars, *operands)


def _finish_body(frame_ref, span_ref, counts_ref, q_ref, k_ref, v_ref, acc_in, top_in, packed, out_ref, acc, top):
    acc[...] = acc_in[...]
    top[...] = top_in[...]
    limit = _visible(frame_ref[0], 0, WIN - 1, span_ref, counts_ref)
    limit = jnp.where(frame_ref[0] % 2 == 0, limit, 0)
    _attend(limit, q_ref, k_ref, v_ref, acc, top)
    own_top, other_top = top[0], packed[0, :, HD : HD + 1]
    own_total, other_total = acc[0, :, HD:], packed[0, :, 2 * HD - 1 :]
    both_top = jnp.maximum(own_top, other_top)
    own_part = jnp.exp2((own_top - both_top) * EXP2_SCALE)
    other_part = jnp.exp2((other_top - both_top) * EXP2_SCALE)
    total = own_total * own_part + other_total * other_part
    mixed = acc[0, :, :HD] * own_part + packed[0, :, :HD] * other_part
    out_ref[...] = (mixed / total).astype(jnp.bfloat16)


def finish_call(scalars, q_own, source, state, packed, head0, heads, name):
    per_frame = q_own.shape[0]
    acc_spec = pl.BlockSpec((1, per_frame, 2 * HD), lambda h, *_: (h, 0, 0))
    top_spec = pl.BlockSpec((1, per_frame, HD), lambda h, *_: (h, 0, 0))
    pairs = heads * per_frame * per_frame
    return pl.pallas_call(
        _finish_body,
        out_shape=jax.ShapeDtypeStruct((per_frame, heads * HD), jnp.bfloat16),
        grid_spec=pltpu.PrefetchScalarGridSpec(
            num_scalar_prefetch=3,
            grid=(heads,),
            in_specs=[
                pl.BlockSpec((per_frame, HD), lambda h, *_: (0, head0 + h)),
                pl.BlockSpec((per_frame, HD), lambda h, *_: (0, h)),
                pl.BlockSpec((per_frame, HD), lambda h, *_: (0, heads + h)),
                acc_spec,
                top_spec,
                acc_spec,
            ],
            out_specs=pl.BlockSpec((per_frame, HD), lambda h, *_: (0, h)),
            scratch_shapes=[
                pltpu.VMEM((1, per_frame, 2 * HD), jnp.float32),
                pltpu.VMEM((1, per_frame, HD), jnp.float32),
            ],
        ),
        cost_estimate=pl.CostEstimate(
            flops=pairs * HD * 8, transcendentals=pairs, bytes_accessed=per_frame * HD * 16 * heads
        ),
        compiler_params=pltpu.CompilerParams(vmem_limit_bytes=40 << 20),
        name=name,
    )(*scalars, q_own, source, source, *state, packed)


def _copy_body(in_ref, out_ref):
    out_ref[0] = in_ref[...]


def column_blocks(weight, groups):
    rows, width = weight.shape
    columns = width // groups
    return pl.pallas_call(
        _copy_body,
        out_shape=jax.ShapeDtypeStruct((groups, rows, columns), weight.dtype),
        grid=(groups,),
        in_specs=[pl.BlockSpec((rows, columns), lambda g: (0, g))],
        out_specs=pl.BlockSpec((1, rows, columns), lambda g: (g, 0, 0)),
        name="column_blocks",
    )(weight)


def _project_body(groups, row0, width, has_base):
    def body(*refs):
        if has_base:
            base_ref, a_ref, w_ref, out_ref = refs
            total = base_ref[...]
        else:
            a_ref, w_ref, out_ref = refs
            total = None
        for group in range(groups):
            part = jnp.dot(
                a_ref[group], w_ref[group, row0 : row0 + width, :], preferred_element_type=jnp.float32
            )
            total = part if total is None else total + part
        out_ref[...] = total.astype(out_ref.dtype)

    return body


def project_call(base, gathered, weight, row0, dtype, name, block=128):
    groups, per_frame, width = gathered.shape
    columns = weight.shape[2]
    rows = pl.BlockSpec((block, columns), lambda r: (r, 0))
    in_specs = [
        pl.BlockSpec((groups, block, width), lambda r: (0, r, 0)),
        pl.BlockSpec(weight.shape, lambda r: (0, 0, 0)),
    ]
    operands = [gathered, weight]
    if base is not None:
        in_specs.insert(0, rows)
        operands.insert(0, base)
    flops = 2 * groups * per_frame * width * columns
    return pl.pallas_call(
        _project_body(groups, row0, width, base is not None),
        out_shape=jax.ShapeDtypeStruct((per_frame, columns), dtype),
        grid=(per_frame // block,),
        in_specs=in_specs,
        out_specs=rows,
        cost_estimate=pl.CostEstimate(flops=flops, transcendentals=0, bytes_accessed=4 << 20),
        compiler_params=pltpu.CompilerParams(vmem_limit_bytes=40 << 20),
        name=name,
    )(*operands)


def on_device(queries, keys, values, out_weight, span, counts):
    per_frame, head_width = queries.shape
    frames = lax.axis_size("frame")
    groups = lax.axis_size("head")
    frame = lax.axis_index("frame").astype(jnp.int32).reshape(1)
    scalars = (frame, span, counts)
    swap = [(i, i ^ 1) for i in range(frames)]
    by_chip = [(i, i + 2) for i in range(frames - 2)]
    to_even = [(i, i + 1) for i in range(1, frames - 1, 2)]
    after = lax.optimization_barrier

    def send(block, route):
        return lax.ppermute(block, "frame", route)

    def pack(lo, hi):
        return jnp.concatenate([keys[:, lo:hi], values[:, lo:hi]], axis=1)

    def attend_a(sources, hops, state, hand_over, name):
        return attention_call(scalars, queries, q_other, sources, hops, state, 0, 2, hand_over, name)

    def attend_b(sources, hops, state, hand_over, name):
        return attention_call(scalars, queries, q_other, sources, hops, state, 2, 1, hand_over, name)

    a0 = pack(0, 2 * HD)
    a1 = send(a0, by_chip)
    q_other = send(queries, swap)
    blocks = column_blocks(out_weight, groups)
    weight = lax.all_to_all(blocks, "head", split_axis=0, concat_axis=0, tiled=True)
    b0 = pack(2 * HD, 3 * HD)

    a1, q_other, b0, blocks = after((a1, q_other, b0, blocks))
    a2 = send(a1, by_chip)
    b1 = send(b0, by_chip)
    state_a = attend_a([a0, a1], (0, 1), None, False, "attend_a01")

    a2, b1, state_a = after((a2, b1, state_a))
    a3 = send(a2, by_chip)
    b2 = send(b1, by_chip)
    state_a = attend_a([a2], (2,), state_a, False, "attend_a2")
    state_b = attend_b([b0, b1], (0, 1), None, False, "attend_b01")

    a3, b2, state_a, state_b = after((a3, b2, state_a, state_b))
    a4 = send(a3, to_even)
    *own_a, packed_a = attend_a([a3], (3,), state_a, True, "attend_a3")
    from_other_a = send(packed_a, swap)
    b2, packed_a = after((b2, packed_a))
    b3 = send(b2, by_chip)
    state_b = attend_b([b2], (2,), state_b, False, "attend_b2")
    attended_a = finish_call(scalars, queries, a4, own_a, from_other_a, 0, 2, "finish_a")
    gathered_a = lax.all_gather(attended_a, "head", axis=0, tiled=False)

    b4 = send(b3, to_even)
    *own_b, packed_b = attend_b([b3], (3,), state_b, True, "attend_b3")
    from_other_b = send(packed_b, swap)
    attended_b = finish_call(scalars, queries, b4, own_b, from_other_b, 2, 1, "finish_b")
    gathered_b = lax.all_to_all(
        jnp.broadcast_to(attended_b[None], (groups, per_frame, HD)),
        "head", split_axis=0, concat_axis=0, tiled=True,
    )
    base = project_call(None, gathered_b, weight, 2 * HD, jnp.float32, "project_b")
    return project_call(base, gathered_a, weight, 0, jnp.bfloat16, "project_a")


def solution(mesh):
    return jax.shard_map(
        on_device,
        mesh=mesh,
        in_specs=(
            P("frame", "head"),
            P("frame", "head"),
            P("frame", "head"),
            P("head", None),
            P(),
            P(),
        ),
        out_specs=P("frame", "head"),
        check_vma=False,
    )
```

```python
import jax
import jax.numpy as jnp
from jax import lax
from jax.experimental import pallas as pl
from jax.experimental.pallas import tpu as pltpu
from jax.sharding import PartitionSpec as P

HD = 128
WIN = 8
NEG = -1e30
EXP2_SCALE = HD ** (-0.5) * 1.4426950408889634
ROW_BLOCK = 256
SMALL_VMEM = 16 << 20
LARGE_VMEM = 24 << 20
BRIEF = pl.CostEstimate(flops=1, transcendentals=0, bytes_accessed=1)


def _attend(limit, q_ref, k_ref, v_ref, acc_ref, top_ref):
    slots = k_ref.shape[0]

    @pl.when(limit > 0)
    def _():
        keys = k_ref[...]
        values = jnp.concatenate([v_ref[...], jnp.ones((slots, HD), jnp.bfloat16)], axis=1)
        slot = lax.broadcasted_iota(jnp.int32, (1, slots), 1)
        hidden = jnp.where(slot < limit, 0.0, NEG)
        for start in range(0, q_ref.shape[0], ROW_BLOCK):
            rows = pl.ds(start, ROW_BLOCK)
            scores = lax.dot_general(
                q_ref[rows, :], keys, (((1,), (1,)), ((), ())), preferred_element_type=jnp.float32
            )
            scores = scores + hidden
            old_top = top_ref[0, rows, :]
            new_top = jnp.maximum(old_top, jnp.max(scores, axis=1, keepdims=True))
            wide_top = jnp.tile(new_top, (1, slots // HD))
            weights = jnp.exp2((scores - wide_top) * EXP2_SCALE).astype(jnp.bfloat16)
            rescale = jnp.exp2((old_top - new_top) * EXP2_SCALE)
            acc_ref[0, rows, :] = acc_ref[0, rows, :] * jnp.tile(rescale, (1, 2)) + jnp.dot(
                weights, values, preferred_element_type=jnp.float32
            )
            top_ref[0, rows, :] = new_top


def _visible(frame, side, behind, span_ref, counts_ref):
    query = frame if side == 0 else frame + 1 - 2 * (frame % 2)
    source = frame - behind
    back = query - source
    seen = (source >= 0) & (back >= 0) & (back < span_ref[query])
    return jnp.where(seen, counts_ref[jnp.maximum(source, 0)], 0)


def in_hbm(array):
    return pltpu.with_memory_space_constraint(array, pltpu.HBM)


def _start(acc, top):
    acc[...] = jnp.zeros_like(acc)
    top[...] = jnp.full_like(top, NEG)


def _attention_body(hops, first, hand_over):
    def body(frame_ref, span_ref, counts_ref, *refs):
        refs = list(refs)
        q_refs = [refs.pop(0), refs.pop(0)]
        kv_refs = [(refs.pop(0), refs.pop(0)) for _ in hops]
        if first:
            state_in = None
        else:
            state_in = [refs.pop(0) for _ in range(4)]
        if hand_over:
            own_acc, own_top, packed, other_acc, other_top = refs
        else:
            own_acc, own_top, other_acc, other_top = refs
        state = (own_acc, own_top, other_acc, other_top)
        if first:
            _start(own_acc, own_top)
            _start(other_acc, other_top)
        else:
            for ref, ref_in in zip(state, state_in):
                ref[...] = ref_in[...]
        frame = frame_ref[0]
        for hop, (k_ref, v_ref) in zip(hops, kv_refs):
            for side in (0, 1):
                limit = _visible(frame, side, 2 * hop, span_ref, counts_ref)
                _attend(limit, q_refs[side], k_ref, v_ref, state[2 * side], state[2 * side + 1])
        if hand_over:
            lane = lax.broadcasted_iota(jnp.int32, (1, HD), 1)
            packed[0, :, :HD] = other_acc[0, :, :HD]
            packed[0, :, HD:] = jnp.where(lane < HD // 2, other_top[0], other_acc[0, :, HD:])

    return body


def attention_call(scalars, q_own, q_other, sources, hops, state, hand_over, name):
    per_frame, width = q_own.shape
    heads = width // HD
    first = state is None
    column = pl.BlockSpec((per_frame, HD), lambda h, *_: (0, h))
    acc_spec = pl.BlockSpec((1, per_frame, 2 * HD), lambda h, *_: (h, 0, 0))
    top_spec = pl.BlockSpec((1, per_frame, HD), lambda h, *_: (h, 0, 0))
    in_specs = [column, column]
    operands = [q_own, q_other]
    for keys_and_values in sources:
        in_specs += [column, column]
        operands += keys_and_values
    if not first:
        in_specs += [acc_spec, top_spec] * 2
        operands += [in_hbm(x) for x in state]
    acc_shape = jax.ShapeDtypeStruct((heads, per_frame, 2 * HD), jnp.float32)
    top_shape = jax.ShapeDtypeStruct((heads, per_frame, HD), jnp.float32)
    scratch = []
    if hand_over:
        out_specs = [acc_spec, top_spec, acc_spec]
        out_shape = [acc_shape, top_shape, acc_shape]
        scratch = [
            pltpu.VMEM((1, per_frame, 2 * HD), jnp.float32),
            pltpu.VMEM((1, per_frame, HD), jnp.float32),
        ]
    else:
        out_specs = [acc_spec, top_spec] * 2
        out_shape = [pltpu.HBM(s.shape, s.dtype) for s in [acc_shape, top_shape] * 2]
    return pl.pallas_call(
        _attention_body(hops, first, hand_over),
        out_shape=out_shape,
        grid_spec=pltpu.PrefetchScalarGridSpec(
            num_scalar_prefetch=3,
            grid=(heads,),
            in_specs=in_specs,
            out_specs=out_specs,
            scratch_shapes=scratch,
        ),
        cost_estimate=BRIEF,
        compiler_params=pltpu.CompilerParams(vmem_limit_bytes=SMALL_VMEM),
        name=name,
    )(*scalars, *operands)


def _finish_body(frame_ref, span_ref, counts_ref, q_ref, k_ref, v_ref, acc_in, top_in, packed, upper_ref, lower_ref, acc, top):
    acc[...] = acc_in[...]
    top[...] = top_in[...]
    limit = _visible(frame_ref[0], 0, WIN - 1, span_ref, counts_ref)
    limit = jnp.where(frame_ref[0] % 2 == 0, limit, 0)
    _attend(limit, q_ref, k_ref, v_ref, acc, top)
    own_top, other_top = top[0], packed[0, :, HD : HD + 1]
    own_total, other_total = acc[0, :, HD:], packed[0, :, 2 * HD - 1 :]
    both_top = jnp.maximum(own_top, other_top)
    own_part = jnp.exp2((own_top - both_top) * EXP2_SCALE)
    other_part = jnp.exp2((other_top - both_top) * EXP2_SCALE)
    total = own_total * own_part + other_total * other_part
    mixed = acc[0, :, :HD] * own_part + packed[0, :, :HD] * other_part
    mixed = (mixed / total).astype(jnp.bfloat16)
    half = upper_ref.shape[0]
    upper_ref[...] = mixed[:half]
    lower_ref[...] = mixed[half:]


def finish_call(scalars, q_own, keys, values, state, packed, name):
    per_frame, width = q_own.shape
    heads = width // HD
    column = pl.BlockSpec((per_frame, HD), lambda h, *_: (0, h))
    acc_spec = pl.BlockSpec((1, per_frame, 2 * HD), lambda h, *_: (h, 0, 0))
    top_spec = pl.BlockSpec((1, per_frame, HD), lambda h, *_: (h, 0, 0))
    return pl.pallas_call(
        _finish_body,
        out_shape=[jax.ShapeDtypeStruct((per_frame // 2, width), jnp.bfloat16)] * 2,
        grid_spec=pltpu.PrefetchScalarGridSpec(
            num_scalar_prefetch=3,
            grid=(heads,),
            in_specs=[
                column,
                column,
                column,
                acc_spec,
                top_spec,
                acc_spec,
            ],
            out_specs=[pl.BlockSpec((per_frame // 2, HD), lambda h, *_: (0, h))] * 2,
            scratch_shapes=[
                pltpu.VMEM((1, per_frame, 2 * HD), jnp.float32),
                pltpu.VMEM((1, per_frame, HD), jnp.float32),
            ],
        ),
        cost_estimate=BRIEF,
        compiler_params=pltpu.CompilerParams(vmem_limit_bytes=SMALL_VMEM),
        name=name,
    )(*scalars, q_own, keys, values, *state, packed)


def _column_blocks_body(w_ref, out_ref):
    groups, _, columns = out_ref.shape
    for group in range(groups):
        out_ref[group] = w_ref[:, group * columns : (group + 1) * columns]


def column_blocks(weight, groups):
    rows, width = weight.shape
    columns = width // groups
    return pl.pallas_call(
        _column_blocks_body,
        out_shape=pltpu.HBM((groups, rows, columns), weight.dtype),
        grid=(2,),
        in_specs=[pl.BlockSpec((rows // 2, width), lambda r: (r, 0))],
        out_specs=pl.BlockSpec((groups, rows // 2, columns), lambda r: (0, r, 0)),
        cost_estimate=BRIEF,
        compiler_params=pltpu.CompilerParams(vmem_limit_bytes=SMALL_VMEM),
        name="column_blocks",
    )(in_hbm(weight))


def _project_body(places, has_base):
    def body(group_ref, *refs):
        out_ref, w_ref = refs[-1], refs[-2]
        groups, half = w_ref.shape[0], out_ref.shape[0] // 2
        for part in (0, 1):
            rows = pl.ds(part * half, half)
            total = refs[0][rows, :] if has_base else None
            for (place, offset), ref in zip(places, refs[has_base:-2], strict=True):
                if place == part:
                    source = lax.rem(group_ref[0] + offset, groups)
                    product = jnp.dot(ref[...], w_ref[source], preferred_element_type=jnp.float32)
                    total = product if total is None else total + product
            out_ref[rows, :] = total.astype(out_ref.dtype)

    return body


def project_call(group, weight, base, pieces, places, dtype, name):
    groups, height, columns = weight.shape
    half = pieces[0].shape[0]
    operands = ([] if base is None else [base]) + list(pieces) + [weight]
    return pl.pallas_call(
        _project_body(places, base is not None),
        out_shape=jax.ShapeDtypeStruct((2 * half, columns), dtype),
        grid_spec=pltpu.PrefetchScalarGridSpec(
            num_scalar_prefetch=1,
            grid=(1,),
            in_specs=[pl.BlockSpec(x.shape, lambda i, g, n=x.ndim: (0,) * n) for x in operands],
            out_specs=pl.BlockSpec((2 * half, columns), lambda i, g: (0, 0)),
        ),
        cost_estimate=pl.CostEstimate(
            flops=2 * len(pieces) * half * height * columns, transcendentals=0, bytes_accessed=4 << 20
        ),
        compiler_params=pltpu.CompilerParams(vmem_limit_bytes=LARGE_VMEM),
        name=name,
    )(group, *operands)


def on_device(queries, keys, values, out_weight, span, counts):
    per_frame, head_width = queries.shape
    frames = lax.axis_size("frame")
    groups = lax.axis_size("head")
    frame = lax.axis_index("frame").astype(jnp.int32).reshape(1)
    group = lax.axis_index("head").astype(jnp.int32).reshape(1)
    scalars = (frame, span, counts)
    swap = [(i, i ^ 1) for i in range(frames)]
    by_chip = [(i, i + 2) for i in range(frames - 2)]
    to_even = [(i, i + 1) for i in range(1, frames - 1, 2)]
    upward = [(i, (i + 1) % groups) for i in range(groups)]
    downward = [(i, (i - 1) % groups) for i in range(groups)]
    after = lax.optimization_barrier

    def send(block, route, axis="frame"):
        return lax.ppermute(block, axis, route)

    def attend(sources, hops, state, hand_over, name):
        return attention_call(
            scalars, in_hbm(queries), q_other, sources, hops, state, hand_over, name
        )

    k1, v1 = send(keys, by_chip), send(values, by_chip)
    q_other = send(queries, swap)
    blocks, v1 = after((column_blocks(out_weight, groups), v1))
    weight = lax.all_to_all(blocks, "head", split_axis=0, concat_axis=0, tiled=True)
    k2, v2 = send(k1, by_chip), send(v1, by_chip)
    state = attend([(in_hbm(keys), in_hbm(values)), (k1, v1)], (0, 1), None, False, "attend_01")
    k2, v2, state = after((k2, v2, state))
    k3, v3 = send(k2, by_chip), send(v2, by_chip)
    state = attend([(k2, v2)], (2,), state, False, "attend_2")
    k3, v3, state = after((k3, v3, state))
    k4, v4 = send(k3, to_even), send(v3, to_even)
    *own, packed = attend([(k3, v3)], (3,), state, True, "attend_3")
    attended = finish_call(scalars, in_hbm(queries), k4, v4, own, send(packed, swap), "finish")

    def project(base, pieces, places, dtype, name):
        return project_call(group, weight, base, pieces, places, dtype, name)

    up, down = list(attended), list(attended)
    held, places, total = list(attended), ((0, 0), (1, 0)), None
    for step in (1, 2, 3):
        up = [send(block, upward, "head") for block in up]
        down = [send(block, downward, "head") for block in down]
        total = project(total, held, places, jnp.float32, f"project_{step - 1}")
        held = up + down
        places = ((0, groups - step), (1, groups - step), (0, step), (1, step))
        up[1], down[1], total = after((up[1], down[1], total))
    far = [send(up[0], upward, "head"), send(down[1], downward, "head")]
    total = project(total, held, places, jnp.float32, "project_3")
    return project(total, far, ((0, 4), (1, 4)), jnp.bfloat16, "project_4")


def solution(mesh):
    return jax.shard_map(
        on_device,
        mesh=mesh,
        in_specs=(
            P("frame", "head"),
            P("frame", "head"),
            P("frame", "head"),
            P("head", None),
            P(),
            P(),
        ),
        out_specs=P("frame", "head"),
        check_vma=False,
    )
```

```python
import jax
import jax.numpy as jnp
from jax import lax
from jax.experimental import pallas as pl
from jax.experimental.pallas import tpu as pltpu
from jax.sharding import PartitionSpec as P

HD = 128
WIN = 8
NEG = -1e30
EXP2_SCALE = HD ** (-0.5) * 1.4426950408889634
ROW_BLOCK = 256
SMALL_VMEM = 16 << 20
LARGE_VMEM = 24 << 20
BRIEF = pl.CostEstimate(flops=1, transcendentals=0, bytes_accessed=1)
LONG = pl.CostEstimate(flops=1 << 34, transcendentals=0, bytes_accessed=1)


def _attend(limit, q_ref, k_ref, v_ref, acc_ref, top_ref):
    slots = k_ref.shape[0]

    @pl.when(limit > 0)
    def _():
        keys = k_ref[...]
        values = jnp.concatenate([v_ref[...], jnp.ones((slots, HD), jnp.bfloat16)], axis=1)
        slot = lax.broadcasted_iota(jnp.int32, (1, slots), 1)
        hidden = jnp.where(slot < limit, 0.0, NEG)
        for start in range(0, q_ref.shape[0], ROW_BLOCK):
            rows = pl.ds(start, ROW_BLOCK)
            scores = lax.dot_general(
                q_ref[rows, :], keys, (((1,), (1,)), ((), ())), preferred_element_type=jnp.float32
            )
            scores = scores + hidden
            old_top = top_ref[0, rows, :]
            new_top = jnp.maximum(old_top, jnp.max(scores, axis=1, keepdims=True))
            wide_top = jnp.tile(new_top, (1, slots // HD))
            weights = jnp.exp2((scores - wide_top) * EXP2_SCALE).astype(jnp.bfloat16)
            rescale = jnp.exp2((old_top - new_top) * EXP2_SCALE)
            acc_ref[0, rows, :] = acc_ref[0, rows, :] * jnp.tile(rescale, (1, 2)) + jnp.dot(
                weights, values, preferred_element_type=jnp.float32
            )
            top_ref[0, rows, :] = new_top


def _visible(frame, side, behind, span_ref, counts_ref):
    query = frame if side == 0 else frame + 1 - 2 * (frame % 2)
    source = frame - behind
    back = query - source
    seen = (source >= 0) & (back >= 0) & (back < span_ref[query])
    return jnp.where(seen, counts_ref[jnp.maximum(source, 0)], 0)


def in_hbm(array):
    return pltpu.with_memory_space_constraint(array, pltpu.HBM)


def _unpack(packed, acc, top):
    acc[0, :, :HD] = packed[0, :, :HD]
    acc[0, :, HD:] = jnp.broadcast_to(packed[0, :, 2 * HD - 1 :], (acc.shape[1], HD))
    top[0] = jnp.broadcast_to(packed[0, :, HD : HD + 1], (acc.shape[1], HD))


def _attention_body(sides, hops, first):
    def body(frame_ref, span_ref, counts_ref, *refs):
        refs = list(refs)
        take = lambda n: [refs.pop(0) for _ in range(n)]
        q_refs = take(len(sides))
        kv_refs = [take(2) for _ in hops]
        state_refs = [None] * len(sides) if first else take(len(sides))
        out_refs = take(len(sides))
        scratch = [take(2) for _ in sides]
        frame = frame_ref[0]
        for state, (acc, top) in zip(state_refs, scratch):
            if first:
                acc[...] = jnp.zeros_like(acc)
                top[...] = jnp.full_like(top, NEG)
            else:
                _unpack(state, acc, top)
        for hop, (k_ref, v_ref) in zip(hops, kv_refs):
            for side, q_ref, (acc, top) in zip(sides, q_refs, scratch):
                limit = _visible(frame, side, 2 * hop, span_ref, counts_ref)
                _attend(limit, q_ref, k_ref, v_ref, acc, top)
        lane = lax.broadcasted_iota(jnp.int32, (1, HD), 1)
        for out, (acc, top) in zip(out_refs, scratch):
            out[0, :, :HD] = acc[0, :, :HD]
            out[0, :, HD:] = jnp.where(lane < HD // 2, top[0], acc[0, :, HD:])

    return body


def _specs(per_frame):
    column = pl.BlockSpec((per_frame, HD), lambda h, *_: (0, h))
    packed = pl.BlockSpec((1, per_frame, 2 * HD), lambda h, *_: (h, 0, 0))
    scratch = [pltpu.VMEM((1, per_frame, 2 * HD), jnp.float32), pltpu.VMEM((1, per_frame, HD), jnp.float32)]
    return column, packed, scratch


def attention_call(scalars, queries, sources, sides, hops, states, name, cost):
    per_frame, width = queries[0].shape
    heads = width // HD
    column, packed, scratch = _specs(per_frame)
    operands = list(queries) + [array for pair in sources for array in pair] + list(states or ())
    return pl.pallas_call(
        _attention_body(sides, hops, states is None),
        out_shape=[jax.ShapeDtypeStruct((heads, per_frame, 2 * HD), jnp.float32)] * len(sides),
        grid_spec=pltpu.PrefetchScalarGridSpec(
            num_scalar_prefetch=3,
            grid=(heads,),
            in_specs=[column] * (len(sides) + 2 * len(hops)) + [packed] * len(states or ()),
            out_specs=[packed] * len(sides),
            scratch_shapes=scratch * len(sides),
        ),
        cost_estimate=cost,
        compiler_params=pltpu.CompilerParams(vmem_limit_bytes=SMALL_VMEM),
        name=name,
    )(*scalars, *operands)


def _finish_body(frame_ref, span_ref, counts_ref, q_ref, k_ref, v_ref, own, other, upper_ref, lower_ref, acc, top):
    _unpack(own, acc, top)
    limit = _visible(frame_ref[0], 0, WIN - 1, span_ref, counts_ref)
    limit = jnp.where(frame_ref[0] % 2 == 0, limit, 0)
    _attend(limit, q_ref, k_ref, v_ref, acc, top)
    own_top, other_top = top[0], other[0, :, HD : HD + 1]
    own_total, other_total = acc[0, :, HD:], other[0, :, 2 * HD - 1 :]
    both_top = jnp.maximum(own_top, other_top)
    own_part = jnp.exp2((own_top - both_top) * EXP2_SCALE)
    other_part = jnp.exp2((other_top - both_top) * EXP2_SCALE)
    total = own_total * own_part + other_total * other_part
    mixed = acc[0, :, :HD] * own_part + other[0, :, :HD] * other_part
    mixed = (mixed / total).astype(jnp.bfloat16)
    half = upper_ref.shape[0]
    upper_ref[...] = mixed[:half]
    lower_ref[...] = mixed[half:]


def finish_call(scalars, queries, keys, values, own, other, name):
    per_frame, width = queries.shape
    column, packed, scratch = _specs(per_frame)
    return pl.pallas_call(
        _finish_body,
        out_shape=[jax.ShapeDtypeStruct((per_frame // 2, width), jnp.bfloat16)] * 2,
        grid_spec=pltpu.PrefetchScalarGridSpec(
            num_scalar_prefetch=3,
            grid=(width // HD,),
            in_specs=[column, column, column, packed, packed],
            out_specs=[pl.BlockSpec((per_frame // 2, HD), lambda h, *_: (0, h))] * 2,
            scratch_shapes=scratch,
        ),
        cost_estimate=BRIEF,
        compiler_params=pltpu.CompilerParams(vmem_limit_bytes=SMALL_VMEM),
        name=name,
    )(*scalars, queries, keys, values, own, other)


def in_hbm(array):
    return pltpu.with_memory_space_constraint(array, pltpu.HBM)


def _column_blocks_body(w_ref, out_ref):
    groups, _, columns = out_ref.shape
    for group in range(groups):
        out_ref[group] = w_ref[:, group * columns : (group + 1) * columns]


def column_blocks(weight, groups):
    rows, width = weight.shape
    columns = width // groups
    return pl.pallas_call(
        _column_blocks_body,
        out_shape=pltpu.HBM((groups, rows, columns), weight.dtype),
        grid=(2,),
        in_specs=[pl.BlockSpec((rows // 2, width), lambda r: (r, 0))],
        out_specs=pl.BlockSpec((groups, rows // 2, columns), lambda r: (0, r, 0)),
        cost_estimate=BRIEF,
        compiler_params=pltpu.CompilerParams(vmem_limit_bytes=SMALL_VMEM),
        name="column_blocks",
    )(in_hbm(weight))


def _project_body(places, has_base):
    def body(group_ref, *refs):
        out_ref, w_ref = refs[-1], refs[-2]
        groups, half = w_ref.shape[0], out_ref.shape[0] // 2
        for part in (0, 1):
            rows = pl.ds(part * half, half)
            total = refs[0][rows, :] if has_base else None
            for (place, offset), ref in zip(places, refs[has_base:-2], strict=True):
                if place == part:
                    source = lax.rem(group_ref[0] + offset, groups)
                    product = jnp.dot(ref[...], w_ref[source], preferred_element_type=jnp.float32)
                    total = product if total is None else total + product
            out_ref[rows, :] = total.astype(out_ref.dtype)

    return body


def project_call(group, weight, base, pieces, places, dtype, name):
    groups, height, columns = weight.shape
    half = pieces[0].shape[0]
    operands = ([] if base is None else [base]) + list(pieces) + [weight]
    return pl.pallas_call(
        _project_body(places, base is not None),
        out_shape=jax.ShapeDtypeStruct((2 * half, columns), dtype),
        grid_spec=pltpu.PrefetchScalarGridSpec(
            num_scalar_prefetch=1,
            grid=(1,),
            in_specs=[pl.BlockSpec(x.shape, lambda i, g, n=x.ndim: (0,) * n) for x in operands],
            out_specs=pl.BlockSpec((2 * half, columns), lambda i, g: (0, 0)),
        ),
        cost_estimate=pl.CostEstimate(
            flops=2 * len(pieces) * half * height * columns, transcendentals=0, bytes_accessed=4 << 20
        ),
        compiler_params=pltpu.CompilerParams(vmem_limit_bytes=LARGE_VMEM),
        name=name,
    )(group, *operands)


def on_device(queries, keys, values, out_weight, span, counts):
    per_frame, head_width = queries.shape
    frames = lax.axis_size("frame")
    groups = lax.axis_size("head")
    frame = lax.axis_index("frame").astype(jnp.int32).reshape(1)
    group = lax.axis_index("head").astype(jnp.int32).reshape(1)
    scalars = (frame, span, counts)
    swap = [(i, i ^ 1) for i in range(frames)]
    by_chip = [(i, i + 2) for i in range(frames - 2)]
    to_even = [(i, i + 1) for i in range(1, frames - 1, 2)]
    upward = [(i, (i + 1) % groups) for i in range(groups)]
    downward = [(i, (i - 1) % groups) for i in range(groups)]
    after = lax.optimization_barrier

    def send(block, route, axis="frame"):
        return lax.ppermute(block, axis, route)

    def attend(sources, sides, hops, states, name, cost=BRIEF):
        both = (in_hbm(queries), q_other)
        return attention_call(
            scalars, [both[side] for side in sides], sources, sides, hops, states, name, cost
        )

    k1, v1 = send(keys, by_chip), send(values, by_chip)
    q_other = send(queries, swap)
    k2, v2 = send(k1, by_chip), send(v1, by_chip)
    near = [(in_hbm(keys), in_hbm(values)), (k1, v1)]
    own, other = attend(near, (0, 1), (0, 1), None, "attend_01", LONG)
    blocks = column_blocks(out_weight, groups)
    weight = lax.all_to_all(blocks, "head", split_axis=0, concat_axis=0, tiled=True)
    k3, v3 = send(k2, by_chip), send(v2, by_chip)
    own, other = attend([(k2, v2)], (0, 1), (2,), [own, other], "attend_2", LONG)
    k3, v3, own, other = after((k3, v3, own, other))
    (other,) = attend([(k3, v3)], (1,), (3,), [other], "attend_3_other")
    from_other = send(other, swap)
    k4, v4 = send(k3, to_even), send(v3, to_even)
    (own,) = attend([(k3, v3)], (0,), (3,), [own], "attend_3_own", LONG)
    attended = finish_call(scalars, in_hbm(queries), k4, v4, own, from_other, "finish")

    def project(base, pieces, places, dtype, name):
        return project_call(group, weight, base, pieces, places, dtype, name)

    up, down = list(attended), list(attended)
    held, places, total = list(attended), ((0, 0), (1, 0)), None
    for step in (1, 2, 3):
        up = [send(block, upward, "head") for block in up]
        down = [send(block, downward, "head") for block in down]
        total = project(total, held, places, jnp.float32, f"project_{step - 1}")
        held = up + down
        places = ((0, groups - step), (1, groups - step), (0, step), (1, step))
        up[1], down[1], total = after((up[1], down[1], total))
    far = [send(up[0], upward, "head"), send(down[1], downward, "head")]
    total = project(total, held, places, jnp.float32, "project_3")
    return project(total, far, ((0, 4), (1, 4)), jnp.bfloat16, "project_4")


def solution(mesh):
    return jax.shard_map(
        on_device,
        mesh=mesh,
        in_specs=(
            P("frame", "head"),
            P("frame", "head"),
            P("frame", "head"),
            P("head", None),
            P(),
            P(),
        ),
        out_specs=P("frame", "head"),
        check_vma=False,
    )
```

```python
import jax
import jax.numpy as jnp
from jax import lax
from jax.experimental import pallas as pl
from jax.experimental.pallas import tpu as pltpu
from jax.sharding import PartitionSpec as P

HD = 128
WIN = 8
NEG = -1e30
EXP2_SCALE = HD ** (-0.5) * 1.4426950408889634
ROW_BLOCK = 256
SMALL_VMEM = 16 << 20
LARGE_VMEM = 24 << 20
BRIEF = pl.CostEstimate(flops=1, transcendentals=0, bytes_accessed=1)
LONG = pl.CostEstimate(flops=1 << 34, transcendentals=0, bytes_accessed=1)


def _attend(limit, q_ref, k_ref, v_ref, acc_ref, top_ref):
    slots = k_ref.shape[0]

    @pl.when(limit > 0)
    def _():
        keys = k_ref[...]
        values = jnp.concatenate([v_ref[...], jnp.ones((slots, HD), jnp.bfloat16)], axis=1)
        slot = lax.broadcasted_iota(jnp.int32, (1, slots), 1)
        hidden = jnp.where(slot < limit, 0.0, NEG)
        for start in range(0, q_ref.shape[0], ROW_BLOCK):
            rows = pl.ds(start, ROW_BLOCK)
            scores = lax.dot_general(
                q_ref[rows, :], keys, (((1,), (1,)), ((), ())), preferred_element_type=jnp.float32
            )
            scores = scores + hidden
            old_top = top_ref[0, rows, :]
            new_top = jnp.maximum(old_top, jnp.max(scores, axis=1, keepdims=True))
            wide_top = jnp.tile(new_top, (1, slots // HD))
            weights = jnp.exp2((scores - wide_top) * EXP2_SCALE).astype(jnp.bfloat16)
            rescale = jnp.exp2((old_top - new_top) * EXP2_SCALE)
            acc_ref[0, rows, :] = acc_ref[0, rows, :] * jnp.tile(rescale, (1, 2)) + jnp.dot(
                weights, values, preferred_element_type=jnp.float32
            )
            top_ref[0, rows, :] = new_top


def _visible(frame, side, behind, span_ref, counts_ref):
    query = frame if side == 0 else frame + 1 - 2 * (frame % 2)
    source = frame - behind
    back = query - source
    seen = (source >= 0) & (back >= 0) & (back < span_ref[query])
    return jnp.where(seen, counts_ref[jnp.maximum(source, 0)], 0)


def _unpack(packed, acc, top):
    acc[0, :, :HD] = packed[0, :, :HD]
    acc[0, :, HD:] = jnp.broadcast_to(packed[0, :, 2 * HD - 1 :], (acc.shape[1], HD))
    top[0] = jnp.broadcast_to(packed[0, :, HD : HD + 1], (acc.shape[1], HD))


def _attention_body(sides, hops, first):
    def body(frame_ref, span_ref, counts_ref, *refs):
        refs = list(refs)
        take = lambda n: [refs.pop(0) for _ in range(n)]
        q_refs = take(len(sides))
        kv_refs = [take(2) for _ in hops]
        state_refs = [None] * len(sides) if first else take(len(sides))
        out_refs = take(len(sides))
        scratch = [take(2) for _ in sides]
        frame = frame_ref[0]
        for state, (acc, top) in zip(state_refs, scratch):
            if first:
                acc[...] = jnp.zeros_like(acc)
                top[...] = jnp.full_like(top, NEG)
            else:
                _unpack(state, acc, top)
        for hop, (k_ref, v_ref) in zip(hops, kv_refs):
            for side, q_ref, (acc, top) in zip(sides, q_refs, scratch):
                limit = _visible(frame, side, 2 * hop, span_ref, counts_ref)
                _attend(limit, q_ref, k_ref, v_ref, acc, top)
        lane = lax.broadcasted_iota(jnp.int32, (1, HD), 1)
        for out, (acc, top) in zip(out_refs, scratch):
            out[0, :, :HD] = acc[0, :, :HD]
            out[0, :, HD:] = jnp.where(lane < HD // 2, top[0], acc[0, :, HD:])

    return body


def _plane(array, plane):
    if array.ndim == 2:
        return pl.BlockSpec((array.shape[0], HD), lambda h, *_: (0, h))
    return pl.BlockSpec((None, array.shape[1], HD), lambda h, *_: (plane, 0, h))


def _specs(per_frame, head0):
    column = pl.BlockSpec((per_frame, HD), lambda h, *_: (0, head0 + h))
    packed = pl.BlockSpec((1, per_frame, 2 * HD), lambda h, *_: (h, 0, 0))
    scratch = [pltpu.VMEM((1, per_frame, 2 * HD), jnp.float32), pltpu.VMEM((1, per_frame, HD), jnp.float32)]
    return column, packed, scratch


def attention_call(scalars, queries, head0, heads, sources, sides, hops, states, name, cost):
    per_frame = queries[0].shape[0]
    column, packed, scratch = _specs(per_frame, head0)
    operands = list(queries) + [source for source in sources for _ in (0, 1)] + list(states or ())
    planes = [_plane(source, plane) for source in sources for plane in (0, 1)]
    return pl.pallas_call(
        _attention_body(sides, hops, states is None),
        out_shape=[jax.ShapeDtypeStruct((heads, per_frame, 2 * HD), jnp.float32)] * len(sides),
        grid_spec=pltpu.PrefetchScalarGridSpec(
            num_scalar_prefetch=3,
            grid=(heads,),
            in_specs=[column] * len(sides) + planes + [packed] * len(states or ()),
            out_specs=[packed] * len(sides),
            scratch_shapes=scratch * len(sides),
        ),
        cost_estimate=cost,
        compiler_params=pltpu.CompilerParams(vmem_limit_bytes=SMALL_VMEM),
        name=name,
    )(*scalars, *operands)


def _finish_body(frame_ref, span_ref, counts_ref, q_ref, k_ref, v_ref, own, other, out_ref, acc, top):
    _unpack(own, acc, top)
    limit = _visible(frame_ref[0], 0, WIN - 1, span_ref, counts_ref)
    limit = jnp.where(frame_ref[0] % 2 == 0, limit, 0)
    _attend(limit, q_ref, k_ref, v_ref, acc, top)
    own_top, other_top = top[0], other[0, :, HD : HD + 1]
    own_total, other_total = acc[0, :, HD:], other[0, :, 2 * HD - 1 :]
    both_top = jnp.maximum(own_top, other_top)
    own_part = jnp.exp2((own_top - both_top) * EXP2_SCALE)
    other_part = jnp.exp2((other_top - both_top) * EXP2_SCALE)
    total = own_total * own_part + other_total * other_part
    mixed = acc[0, :, :HD] * own_part + other[0, :, :HD] * other_part
    out_ref[...] = (mixed / total).astype(jnp.bfloat16)


def finish_call(scalars, queries, head0, keys, values, own, other, name):
    heads, per_frame, _ = own.shape
    column, packed, scratch = _specs(per_frame, head0)
    return pl.pallas_call(
        _finish_body,
        out_shape=jax.ShapeDtypeStruct((per_frame, heads * HD), jnp.bfloat16),
        grid_spec=pltpu.PrefetchScalarGridSpec(
            num_scalar_prefetch=3,
            grid=(heads,),
            in_specs=[column, _plane(keys, 0), _plane(values, 1), packed, packed],
            out_specs=pl.BlockSpec((per_frame, HD), lambda h, *_: (0, h)),
            scratch_shapes=scratch,
        ),
        cost_estimate=BRIEF,
        compiler_params=pltpu.CompilerParams(vmem_limit_bytes=SMALL_VMEM),
        name=name,
    )(*scalars, queries, keys, values, own, other)


def _pack_body(first, k_ref, v_ref, a_ref, b_ref):
    for plane, ref in enumerate((k_ref, v_ref)):
        a_ref[plane] = ref[:, :first]
        b_ref[plane] = ref[:, first:]


def pack_call(keys, values, first):
    per_frame, width = keys.shape
    return pl.pallas_call(
        lambda *refs: _pack_body(first, *refs),
        out_shape=[
            jax.ShapeDtypeStruct((2, per_frame, first), keys.dtype),
            jax.ShapeDtypeStruct((2, per_frame, width - first), keys.dtype),
        ],
        cost_estimate=BRIEF,
        compiler_params=pltpu.CompilerParams(vmem_limit_bytes=SMALL_VMEM),
        name="pack",
    )(keys, values)


def in_hbm(array):
    return pltpu.with_memory_space_constraint(array, pltpu.HBM)


def _column_blocks_body(w_ref, out_ref):
    groups, _, columns = out_ref.shape
    for group in range(groups):
        out_ref[group] = w_ref[:, group * columns : (group + 1) * columns]


def column_blocks(weight, groups):
    rows, width = weight.shape
    columns = width // groups
    return pl.pallas_call(
        _column_blocks_body,
        out_shape=pltpu.HBM((groups, rows, columns), weight.dtype),
        grid=(2,),
        in_specs=[pl.BlockSpec((rows // 2, width), lambda r: (r, 0))],
        out_specs=pl.BlockSpec((groups, rows // 2, columns), lambda r: (0, r, 0)),
        cost_estimate=BRIEF,
        compiler_params=pltpu.CompilerParams(vmem_limit_bytes=SMALL_VMEM),
        name="column_blocks",
    )(in_hbm(weight))


def _project_body(places, row0, has_base, has_gathered):
    def body(group_ref, *refs):
        out_ref, w_ref = refs[-1], refs[-2]
        gathered_ref = refs[has_base] if has_gathered else None
        pieces = refs[has_base + has_gathered : -2]
        groups, half = w_ref.shape[0], out_ref.shape[0] // 2
        for part in (0, 1):
            rows = pl.ds(part * half, half)
            total = refs[0][rows, :] if has_base else jnp.zeros((half, out_ref.shape[1]), jnp.float32)
            if has_gathered:
                for source in range(groups):
                    total += jnp.dot(
                        gathered_ref[source, rows, :], w_ref[source, :row0, :], preferred_element_type=jnp.float32
                    )
            for (place, offset), ref in zip(places, pieces, strict=True):
                if place in (part, None):
                    source = lax.rem(group_ref[0] + offset, groups)
                    piece = ref[rows, :] if place is None else ref[...]
                    total += jnp.dot(piece, w_ref[source, row0:, :], preferred_element_type=jnp.float32)
            out_ref[rows, :] = total.astype(out_ref.dtype)

    return body


def project_call(group, weight, row0, base, gathered, pieces, places, dtype, name):
    groups, _, columns = weight.shape
    per_frame = pieces[0].shape[0] * (1 if places[0][0] is None else 2)
    operands = [x for x in (base, gathered) if x is not None] + list(pieces) + [weight]
    return pl.pallas_call(
        _project_body(places, row0, base is not None, gathered is not None),
        out_shape=jax.ShapeDtypeStruct((per_frame, columns), dtype),
        grid_spec=pltpu.PrefetchScalarGridSpec(
            num_scalar_prefetch=1,
            grid=(1,),
            in_specs=[pl.BlockSpec(x.shape, lambda i, g, n=x.ndim: (0,) * n) for x in operands],
            out_specs=pl.BlockSpec((per_frame, columns), lambda i, g: (0, 0)),
        ),
        cost_estimate=pl.CostEstimate(
            flops=len(pieces) * per_frame * weight.shape[1] * columns, transcendentals=0, bytes_accessed=4 << 20
        ),
        compiler_params=pltpu.CompilerParams(vmem_limit_bytes=LARGE_VMEM),
        name=name,
    )(group, *operands)


def on_device(queries, keys, values, out_weight, span, counts):
    per_frame, head_width = queries.shape
    frames = lax.axis_size("frame")
    groups = lax.axis_size("head")
    frame = lax.axis_index("frame").astype(jnp.int32).reshape(1)
    group = lax.axis_index("head").astype(jnp.int32).reshape(1)
    scalars = (frame, span, counts)
    swap = [(i, i ^ 1) for i in range(frames)]
    by_chip = [(i, i + 2) for i in range(frames - 2)]
    to_even = [(i, i + 1) for i in range(1, frames - 1, 2)]
    upward = [(i, (i + 1) % groups) for i in range(groups)]
    downward = [(i, (i - 1) % groups) for i in range(groups)]
    after = lax.optimization_barrier

    def send(block, route, axis="frame"):
        return lax.ppermute(block, axis, route)

    def attend(head0, heads, sources, sides, hops, states, name, cost):
        both = (in_hbm(queries), q_other)
        return attention_call(
            scalars, [both[side] for side in sides], head0, heads, sources, sides, hops, states, name, cost
        )

    a0, b0 = pack_call(keys, values, HD)
    a1, b1 = send(a0, by_chip), send(b0, by_chip)
    q_other = send(queries, swap)
    weight = lax.all_to_all(
        column_blocks(out_weight, groups), "head", split_axis=0, concat_axis=0, tiled=True
    )
    a2 = send(a1, by_chip)
    a2, b1 = after((a2, b1))
    a3, b2 = send(a2, by_chip), send(b1, by_chip)
    states_b = attend(1, 2, [b0, b1], (0, 1), (0, 1), None, "attend_b01", LONG)
    a4 = send(a3, to_even)
    own_a, other_a = attend(0, 1, [a0, a1, a2, a3], (0, 1), (0, 1, 2, 3), None, "attend_a0123", LONG)
    b2, a4, own_a, other_a, states_b = after((b2, a4, own_a, other_a, states_b))
    b3 = send(b2, by_chip)
    from_other_a = send(other_a, swap)
    own_b, other_b = attend(1, 2, [b2], (0, 1), (2,), states_b, "attend_b2", LONG)
    attended_a = finish_call(scalars, in_hbm(queries), 0, a4, a4, own_a, from_other_a, "finish_a")
    gathered_a = lax.all_to_all(
        jnp.broadcast_to(attended_a[None], (groups, per_frame, HD)),
        "head", split_axis=0, concat_axis=0, tiled=True,
    )
    b3, own_b, other_b, attended_a = after((b3, own_b, other_b, attended_a))
    b4_keys, b4_values = send(b3[0], to_even), send(b3[1], to_even)
    (other_b,) = attend(1, 2, [b3], (1,), (3,), [other_b], "attend_b3_other", BRIEF)
    from_other_b = send(other_b, swap)
    (own_b,) = attend(1, 2, [b3], (0,), (3,), [own_b], "attend_b3_own", BRIEF)
    attended = finish_call(scalars, in_hbm(queries), 1, b4_keys, b4_values, own_b, from_other_b, "finish_b")

    def project(base, gathered, pieces, places, dtype, name):
        return project_call(group, weight, HD, base, gathered, pieces, places, dtype, name)

    half = per_frame // 2
    f32 = jnp.float32
    up1, down1 = send(attended, upward, "head"), send(attended, downward, "head")
    total = project(None, None, [attended], ((None, 0),), f32, "project_0")
    up2, down2 = send(up1, upward, "head"), send(down1, downward, "head")
    total = project(total, gathered_a, [up1, down1], ((None, groups - 1), (None, 1)), f32, "project_1")
    up3 = send(up2, upward, "head")
    down2, total = after((down2, total))
    down3 = send(down2, downward, "head")
    total = project(total, None, [up2, down2], ((None, groups - 2), (None, 2)), f32, "project_2")
    up4 = send(up3[:half], upward, "head")
    down3, total = after((down3, total))
    down4 = send(down3[half:], downward, "head")
    total = project(total, None, [up3, down3], ((None, groups - 3), (None, 3)), f32, "project_3")
    return project(total, None, [up4, down4], ((0, 4), (1, 4)), jnp.bfloat16, "project_4")


def solution(mesh):
    return jax.shard_map(
        on_device,
        mesh=mesh,
        in_specs=(
            P("frame", "head"),
            P("frame", "head"),
            P("frame", "head"),
            P("head", None),
            P(),
            P(),
        ),
        out_specs=P("frame", "head"),
        check_vma=False,
    )
```

```python
import jax
import jax.numpy as jnp
from jax import lax
from jax.experimental import pallas as pl
from jax.experimental.pallas import tpu as pltpu
from jax.sharding import PartitionSpec as P

HD = 128
WIN = 8
NEG = -1e30
EXP2_SCALE = HD ** (-0.5) * 1.4426950408889634
ROW_BLOCK = 256
SMALL_VMEM = 16 << 20
LARGE_VMEM = 24 << 20
BRIEF = pl.CostEstimate(flops=1, transcendentals=0, bytes_accessed=1)
LONG = pl.CostEstimate(flops=1 << 34, transcendentals=0, bytes_accessed=1)


def _attend(limit, q_ref, k_ref, v_ref, acc_ref, top_ref):
    slots = k_ref.shape[0]

    @pl.when(limit > 0)
    def _():
        keys = k_ref[...]
        values = jnp.concatenate([v_ref[...], jnp.ones((slots, HD), jnp.bfloat16)], axis=1)
        slot = lax.broadcasted_iota(jnp.int32, (1, slots), 1)
        hidden = jnp.where(slot < limit, 0.0, NEG)
        for start in range(0, q_ref.shape[0], ROW_BLOCK):
            rows = pl.ds(start, ROW_BLOCK)
            scores = lax.dot_general(
                q_ref[rows, :], keys, (((1,), (1,)), ((), ())), preferred_element_type=jnp.float32
            )
            scores = scores + hidden
            old_top = top_ref[0, rows, :]
            new_top = jnp.maximum(old_top, jnp.max(scores, axis=1, keepdims=True))
            wide_top = jnp.tile(new_top, (1, slots // HD))
            weights = jnp.exp2((scores - wide_top) * EXP2_SCALE).astype(jnp.bfloat16)
            rescale = jnp.exp2((old_top - new_top) * EXP2_SCALE)
            acc_ref[0, rows, :] = acc_ref[0, rows, :] * jnp.tile(rescale, (1, 2)) + jnp.dot(
                weights, values, preferred_element_type=jnp.float32
            )
            top_ref[0, rows, :] = new_top


def _visible(frame, side, behind, span_ref, counts_ref):
    query = frame if side == 0 else frame + 1 - 2 * (frame % 2)
    source = frame - behind
    back = query - source
    seen = (source >= 0) & (back >= 0) & (back < span_ref[query])
    return jnp.where(seen, counts_ref[jnp.maximum(source, 0)], 0)


def _unpack(packed, acc, top):
    acc[0, :, :HD] = packed[0, :, :HD]
    acc[0, :, HD:] = jnp.broadcast_to(packed[0, :, 2 * HD - 1 :], (acc.shape[1], HD))
    top[0] = jnp.broadcast_to(packed[0, :, HD : HD + 1], (acc.shape[1], HD))


def _join(packed, acc, top):
    new_top = jnp.maximum(top[0], packed[0, :, HD : HD + 1])
    own_part = jnp.exp2((top[0] - new_top) * EXP2_SCALE)
    other_part = jnp.exp2((packed[0, :, HD : HD + 1] - new_top) * EXP2_SCALE)
    acc[0, :, :HD] = acc[0, :, :HD] * own_part + packed[0, :, :HD] * other_part
    acc[0, :, HD:] = acc[0, :, HD:] * own_part + packed[0, :, 2 * HD - 1 :] * other_part
    top[0] = new_top


def _attention_body(sides, hops, first):
    def body(frame_ref, span_ref, counts_ref, *refs):
        refs = list(refs)
        take = lambda n: [refs.pop(0) for _ in range(n)]
        q_refs = take(len(sides))
        kv_refs = [take(2) for _ in hops]
        state_refs = [None] * len(sides) if first else take(len(sides))
        out_refs = take(len(sides))
        scratch = [take(2) for _ in sides]
        frame = frame_ref[0]
        for state, (acc, top) in zip(state_refs, scratch):
            if first:
                acc[...] = jnp.zeros_like(acc)
                top[...] = jnp.full_like(top, NEG)
            else:
                _unpack(state, acc, top)
        for hop, (k_ref, v_ref) in zip(hops, kv_refs):
            for side, q_ref, (acc, top) in zip(sides, q_refs, scratch):
                limit = _visible(frame, side, 2 * hop, span_ref, counts_ref)
                _attend(limit, q_ref, k_ref, v_ref, acc, top)
        lane = lax.broadcasted_iota(jnp.int32, (1, HD), 1)
        for out, (acc, top) in zip(out_refs, scratch):
            out[0, :, :HD] = acc[0, :, :HD]
            out[0, :, HD:] = jnp.where(lane < HD // 2, top[0], acc[0, :, HD:])

    return body


def _specs(per_frame):
    column = pl.BlockSpec((per_frame, HD), lambda h, *_: (0, h))
    packed = pl.BlockSpec((1, per_frame, 2 * HD), lambda h, *_: (h, 0, 0))
    scratch = [pltpu.VMEM((1, per_frame, 2 * HD), jnp.float32), pltpu.VMEM((1, per_frame, HD), jnp.float32)]
    return column, packed, scratch


def attention_call(scalars, queries, sources, sides, hops, states, name):
    per_frame, width = queries[0].shape
    heads = width // HD
    column, packed, scratch = _specs(per_frame)
    operands = list(queries) + [array for pair in sources for array in pair] + list(states or ())
    return pl.pallas_call(
        _attention_body(sides, hops, states is None),
        out_shape=[jax.ShapeDtypeStruct((heads, per_frame, 2 * HD), jnp.float32)] * len(sides),
        grid_spec=pltpu.PrefetchScalarGridSpec(
            num_scalar_prefetch=3,
            grid=(heads,),
            in_specs=[column] * (len(sides) + 2 * len(hops)) + [packed] * len(states or ()),
            out_specs=[packed] * len(sides),
            scratch_shapes=scratch * len(sides),
        ),
        cost_estimate=LONG,
        compiler_params=pltpu.CompilerParams(vmem_limit_bytes=SMALL_VMEM),
        name=name,
    )(*scalars, *operands)


def _finish_body(frame_ref, span_ref, counts_ref, q_ref, k_ref, v_ref, own, other, out_ref, acc, top):
    _unpack(own, acc, top)
    limit = _visible(frame_ref[0], 0, WIN - 1, span_ref, counts_ref)
    limit = jnp.where(frame_ref[0] % 2 == 0, limit, 0)
    _attend(limit, q_ref, k_ref, v_ref, acc, top)
    _join(other, acc, top)
    out_ref[...] = (acc[0, :, :HD] / acc[0, :, HD:]).astype(jnp.bfloat16)


def finish_call(scalars, queries, keys, values, own, other, name):
    per_frame, width = queries.shape
    column, packed, scratch = _specs(per_frame)
    return pl.pallas_call(
        _finish_body,
        out_shape=jax.ShapeDtypeStruct((per_frame, width), jnp.bfloat16),
        grid_spec=pltpu.PrefetchScalarGridSpec(
            num_scalar_prefetch=3,
            grid=(width // HD,),
            in_specs=[column, column, column, packed, packed],
            out_specs=column,
            scratch_shapes=scratch,
        ),
        cost_estimate=BRIEF,
        compiler_params=pltpu.CompilerParams(vmem_limit_bytes=SMALL_VMEM),
        name=name,
    )(*scalars, queries, keys, values, own, other)


def in_hbm(array):
    return pltpu.with_memory_space_constraint(array, pltpu.HBM)


def _column_blocks_body(w_ref, out_ref):
    groups, _, columns = out_ref.shape
    for group in range(groups):
        out_ref[group] = w_ref[:, group * columns : (group + 1) * columns]


def column_blocks(weight, groups):
    rows, width = weight.shape
    columns = width // groups
    return pl.pallas_call(
        _column_blocks_body,
        out_shape=pltpu.HBM((groups, rows, columns), weight.dtype),
        grid=(2,),
        in_specs=[pl.BlockSpec((rows // 2, width), lambda r: (r, 0))],
        out_specs=pl.BlockSpec((groups, rows // 2, columns), lambda r: (0, r, 0)),
        cost_estimate=BRIEF,
        compiler_params=pltpu.CompilerParams(vmem_limit_bytes=SMALL_VMEM),
        name="column_blocks",
    )(in_hbm(weight))


def _project_body(places, has_base):
    def body(group_ref, *refs):
        out_ref, w_ref = refs[-1], refs[-2]
        groups, half = w_ref.shape[0], out_ref.shape[0] // 2
        for part in (0, 1):
            rows = pl.ds(part * half, half)
            total = refs[0][rows, :] if has_base else jnp.zeros((half, out_ref.shape[1]), jnp.float32)
            for (place, offset), ref in zip(places, refs[has_base:-2], strict=True):
                if place in (part, None):
                    source = lax.rem(group_ref[0] + offset, groups)
                    piece = ref[rows, :] if place is None else ref[...]
                    total += jnp.dot(piece, w_ref[source], preferred_element_type=jnp.float32)
            out_ref[rows, :] = total.astype(out_ref.dtype)

    return body


def project_call(group, weight, base, pieces, places, dtype, name):
    groups, _, columns = weight.shape
    per_frame = pieces[0].shape[0] * (1 if places[0][0] is None else 2)
    operands = ([] if base is None else [base]) + list(pieces) + [weight]
    return pl.pallas_call(
        _project_body(places, base is not None),
        out_shape=jax.ShapeDtypeStruct((per_frame, columns), dtype),
        grid_spec=pltpu.PrefetchScalarGridSpec(
            num_scalar_prefetch=1,
            grid=(1,),
            in_specs=[pl.BlockSpec(x.shape, lambda i, g, n=x.ndim: (0,) * n) for x in operands],
            out_specs=pl.BlockSpec((per_frame, columns), lambda i, g: (0, 0)),
        ),
        cost_estimate=pl.CostEstimate(
            flops=len(pieces) * per_frame * weight.shape[1] * columns, transcendentals=0, bytes_accessed=4 << 20
        ),
        compiler_params=pltpu.CompilerParams(vmem_limit_bytes=LARGE_VMEM),
        name=name,
    )(group, *operands)


def on_device(queries, keys, values, out_weight, span, counts):
    per_frame, head_width = queries.shape
    frames = lax.axis_size("frame")
    groups = lax.axis_size("head")
    frame = lax.axis_index("frame").astype(jnp.int32).reshape(1)
    group = lax.axis_index("head").astype(jnp.int32).reshape(1)
    scalars = (frame, span, counts)
    swap = [(i, i ^ 1) for i in range(frames)]
    by_chip = [(i, i + 2) for i in range(frames - 2)]
    to_even = [(i, i + 1) for i in range(1, frames - 1, 2)]
    upward = [(i, (i + 1) % groups) for i in range(groups)]
    downward = [(i, (i - 1) % groups) for i in range(groups)]
    after = lax.optimization_barrier

    def send(block, route, axis="frame"):
        return lax.ppermute(block, axis, route)

    def attend(sources, sides, hops, states, name):
        both = (in_hbm(queries), q_other)
        return attention_call(
            scalars, [both[side] for side in sides], sources, sides, hops, states, name
        )

    k1, v1 = send(keys, by_chip), send(values, by_chip)
    q_other = send(queries, swap)
    blocks = column_blocks(out_weight, groups)
    weight = lax.all_to_all(blocks, "head", split_axis=0, concat_axis=0, tiled=True)
    parts = attend([(in_hbm(keys), in_hbm(values))], (0, 1), (0,), None, "attend_0")
    k1, parts = after((k1, parts))
    k2, v2 = send(k1, by_chip), send(v1, by_chip)
    parts = attend([(k1, v1)], (0, 1), (1,), parts, "attend_1")
    k2, parts = after((k2, parts))
    k3, v3 = send(k2, by_chip), send(v2, by_chip)
    own, other = attend([(k2, v2)], (0, 1), (2,), parts, "attend_2")
    k3, v3, own, other = after((k3, v3, own, other))
    (other,) = attend([(k3, v3)], (1,), (3,), [other], "attend_3_other")
    from_other = send(other, swap)
    k4, v4 = send(k3, to_even), send(v3, to_even)
    (own,) = attend([(k3, v3)], (0,), (3,), [own], "attend_3_own")
    attended = finish_call(scalars, in_hbm(queries), k4, v4, own, from_other, "finish")

    def project(base, pieces, places, dtype, name):
        return project_call(group, weight, base, pieces, places, dtype, name)

    half = per_frame // 2
    up, down = attended, attended
    held, places, total = [attended], [(None, 0)], None
    for step in (1, 2, 3):
        up, down = send(up, upward, "head"), send(down, downward, "head")
        total = project(total, held, places, jnp.float32, f"project_{step - 1}")
        held, places = [up, down], [(None, groups - step), (None, step)]
        down, total = after((down, total))
    far = [send(up[:half], upward, "head"), send(down[half:], downward, "head")]
    total = project(total, held, places, jnp.float32, "project_3")
    return project(total, far, [(0, 4), (1, 4)], jnp.bfloat16, "project_4")


def solution(mesh):
    return jax.shard_map(
        on_device,
        mesh=mesh,
        in_specs=(
            P("frame", "head"),
            P("frame", "head"),
            P("frame", "head"),
            P("head", None),
            P(),
            P(),
        ),
        out_specs=P("frame", "head"),
        check_vma=False,
    )
```

```python
import jax
import jax.numpy as jnp
from jax import lax
from jax.experimental import pallas as pl
from jax.experimental.pallas import tpu as pltpu
from jax.sharding import PartitionSpec as P

HD = 128
WIN = 8
NEG = -1e30
EXP2_SCALE = HD ** (-0.5) * 1.4426950408889634
ROW_BLOCK = 256
SMALL_VMEM = 16 << 20
LARGE_VMEM = 24 << 20
BRIEF = pl.CostEstimate(flops=1, transcendentals=0, bytes_accessed=1)
LONG = pl.CostEstimate(flops=1 << 34, transcendentals=0, bytes_accessed=1)


def _attend(limit, q_ref, k_ref, v_ref, acc_ref, top_ref):
    slots = k_ref.shape[0]

    @pl.when(limit > 0)
    def _():
        keys = k_ref[...]
        values = jnp.concatenate([v_ref[...], jnp.ones((slots, HD), jnp.bfloat16)], axis=1)
        slot = lax.broadcasted_iota(jnp.int32, (1, slots), 1)
        hidden = jnp.where(slot < limit, 0.0, NEG)
        for start in range(0, q_ref.shape[0], ROW_BLOCK):
            rows = pl.ds(start, ROW_BLOCK)
            scores = lax.dot_general(
                q_ref[rows, :], keys, (((1,), (1,)), ((), ())), preferred_element_type=jnp.float32
            )
            scores = scores + hidden
            old_top = top_ref[0, rows, :]
            new_top = jnp.maximum(old_top, jnp.max(scores, axis=1, keepdims=True))
            wide_top = jnp.tile(new_top, (1, slots // HD))
            weights = jnp.exp2((scores - wide_top) * EXP2_SCALE).astype(jnp.bfloat16)
            rescale = jnp.exp2((old_top - new_top) * EXP2_SCALE)
            acc_ref[0, rows, :] = acc_ref[0, rows, :] * jnp.tile(rescale, (1, 2)) + jnp.dot(
                weights, values, preferred_element_type=jnp.float32
            )
            top_ref[0, rows, :] = new_top


def _visible(frame, side, behind, span_ref, counts_ref):
    query = frame if side == 0 else frame + 1 - 2 * (frame % 2)
    source = frame - behind
    back = query - source
    seen = (source >= 0) & (back >= 0) & (back < span_ref[query])
    return jnp.where(seen, counts_ref[jnp.maximum(source, 0)], 0)


def _unpack(packed, acc, top):
    acc[0, :, :HD] = packed[0, :, :HD]
    acc[0, :, HD:] = jnp.broadcast_to(packed[0, :, 2 * HD - 1 :], (acc.shape[1], HD))
    top[0] = jnp.broadcast_to(packed[0, :, HD : HD + 1], (acc.shape[1], HD))


def _join(packed, acc, top):
    new_top = jnp.maximum(top[0], packed[0, :, HD : HD + 1])
    own_part = jnp.exp2((top[0] - new_top) * EXP2_SCALE)
    other_part = jnp.exp2((packed[0, :, HD : HD + 1] - new_top) * EXP2_SCALE)
    acc[0, :, :HD] = acc[0, :, :HD] * own_part + packed[0, :, :HD] * other_part
    acc[0, :, HD:] = acc[0, :, HD:] * own_part + packed[0, :, 2 * HD - 1 :] * other_part
    top[0] = new_top


def _attention_body(sides, hop, pieces, first):
    def body(frame_ref, span_ref, counts_ref, *refs):
        refs = list(refs)
        take = lambda n: [refs.pop(0) for _ in range(n)]
        q_refs = take(len(sides))
        kv_refs = [take(2) for _ in range(pieces)]
        state_refs = [None] * len(sides) if first else take(len(sides))
        out_refs = take(len(sides))
        scratch = [take(2) for _ in sides]
        frame = frame_ref[0]
        for state, (acc, top) in zip(state_refs, scratch):
            if first:
                acc[...] = jnp.zeros_like(acc)
                top[...] = jnp.full_like(top, NEG)
            else:
                _unpack(state, acc, top)
        slot0 = 0
        for k_ref, v_ref in kv_refs:
            for side, q_ref, (acc, top) in zip(sides, q_refs, scratch):
                limit = _visible(frame, side, 2 * hop, span_ref, counts_ref)
                _attend(limit - slot0, q_ref, k_ref, v_ref, acc, top)
            slot0 += k_ref.shape[0]
        lane = lax.broadcasted_iota(jnp.int32, (1, HD), 1)
        for out, (acc, top) in zip(out_refs, scratch):
            out[0, :, :HD] = acc[0, :, :HD]
            out[0, :, HD:] = jnp.where(lane < HD // 2, top[0], acc[0, :, HD:])

    return body


def _column(array):
    return pl.BlockSpec((array.shape[0], HD), lambda h, *_: (0, h))


def _specs(per_frame):
    column = pl.BlockSpec((per_frame, HD), lambda h, *_: (0, h))
    packed = pl.BlockSpec((1, per_frame, 2 * HD), lambda h, *_: (h, 0, 0))
    scratch = [pltpu.VMEM((1, per_frame, 2 * HD), jnp.float32), pltpu.VMEM((1, per_frame, HD), jnp.float32)]
    return column, packed, scratch


def attention_call(scalars, queries, sources, sides, hop, states, name):
    per_frame, width = queries[0].shape
    heads = width // HD
    column, packed, scratch = _specs(per_frame)
    operands = list(queries) + [array for pair in sources for array in pair] + list(states or ())
    return pl.pallas_call(
        _attention_body(sides, hop, len(sources), states is None),
        out_shape=[jax.ShapeDtypeStruct((heads, per_frame, 2 * HD), jnp.float32)] * len(sides),
        grid_spec=pltpu.PrefetchScalarGridSpec(
            num_scalar_prefetch=3,
            grid=(heads,),
            in_specs=[column] * len(sides)
            + [_column(array) for pair in sources for array in pair]
            + [packed] * len(states or ()),
            out_specs=[packed] * len(sides),
            scratch_shapes=scratch * len(sides),
        ),
        cost_estimate=LONG,
        compiler_params=pltpu.CompilerParams(vmem_limit_bytes=SMALL_VMEM),
        name=name,
    )(*scalars, *operands)


def _finish_body(frame_ref, span_ref, counts_ref, q_ref, k0_ref, v0_ref, k1_ref, v1_ref, own, other, out_ref, acc, top):
    _unpack(own, acc, top)
    limit = _visible(frame_ref[0], 0, WIN - 1, span_ref, counts_ref)
    limit = jnp.where(frame_ref[0] % 2 == 0, limit, 0)
    _attend(limit, q_ref, k0_ref, v0_ref, acc, top)
    _attend(limit - k0_ref.shape[0], q_ref, k1_ref, v1_ref, acc, top)
    _join(other, acc, top)
    out_ref[...] = (acc[0, :, :HD] / acc[0, :, HD:]).astype(jnp.bfloat16)


def finish_call(scalars, queries, sources, own, other, name):
    per_frame, width = queries.shape
    column, packed, scratch = _specs(per_frame)
    return pl.pallas_call(
        _finish_body,
        out_shape=jax.ShapeDtypeStruct((per_frame, width), jnp.bfloat16),
        grid_spec=pltpu.PrefetchScalarGridSpec(
            num_scalar_prefetch=3,
            grid=(width // HD,),
            in_specs=[column] + [_column(array) for pair in sources for array in pair] + [packed, packed],
            out_specs=column,
            scratch_shapes=scratch,
        ),
        cost_estimate=BRIEF,
        compiler_params=pltpu.CompilerParams(vmem_limit_bytes=SMALL_VMEM),
        name=name,
    )(*scalars, queries, *(array for pair in sources for array in pair), own, other)


def in_hbm(array):
    return pltpu.with_memory_space_constraint(array, pltpu.HBM)


def _column_blocks_body(w_ref, out_ref):
    groups, _, columns = out_ref.shape
    for group in range(groups):
        out_ref[group] = w_ref[:, group * columns : (group + 1) * columns]


def column_blocks(weight, groups):
    rows, width = weight.shape
    columns = width // groups
    return pl.pallas_call(
        _column_blocks_body,
        out_shape=pltpu.HBM((groups, rows, columns), weight.dtype),
        grid=(2,),
        in_specs=[pl.BlockSpec((rows // 2, width), lambda r: (r, 0))],
        out_specs=pl.BlockSpec((groups, rows // 2, columns), lambda r: (0, r, 0)),
        cost_estimate=BRIEF,
        compiler_params=pltpu.CompilerParams(vmem_limit_bytes=SMALL_VMEM),
        name="column_blocks",
    )(in_hbm(weight))


def _project_body(places, has_base):
    def body(group_ref, *refs):
        out_ref, w_ref = refs[-1], refs[-2]
        groups, half = w_ref.shape[0], out_ref.shape[0] // 2
        for part in (0, 1):
            rows = pl.ds(part * half, half)
            total = refs[0][rows, :] if has_base else jnp.zeros((half, out_ref.shape[1]), jnp.float32)
            for (place, offset), ref in zip(places, refs[has_base:-2], strict=True):
                if place in (part, None):
                    source = lax.rem(group_ref[0] + offset, groups)
                    piece = ref[rows, :] if place is None else ref[...]
                    total += jnp.dot(piece, w_ref[source], preferred_element_type=jnp.float32)
            out_ref[rows, :] = total.astype(out_ref.dtype)

    return body


def project_call(group, weight, base, pieces, places, dtype, name):
    groups, _, columns = weight.shape
    per_frame = pieces[0].shape[0] * (1 if places[0][0] is None else 2)
    operands = ([] if base is None else [base]) + list(pieces) + [weight]
    return pl.pallas_call(
        _project_body(places, base is not None),
        out_shape=jax.ShapeDtypeStruct((per_frame, columns), dtype),
        grid_spec=pltpu.PrefetchScalarGridSpec(
            num_scalar_prefetch=1,
            grid=(1,),
            in_specs=[pl.BlockSpec(x.shape, lambda i, g, n=x.ndim: (0,) * n) for x in operands],
            out_specs=pl.BlockSpec((per_frame, columns), lambda i, g: (0, 0)),
        ),
        cost_estimate=pl.CostEstimate(
            flops=len(pieces) * per_frame * weight.shape[1] * columns, transcendentals=0, bytes_accessed=4 << 20
        ),
        compiler_params=pltpu.CompilerParams(vmem_limit_bytes=LARGE_VMEM),
        name=name,
    )(group, *operands)


def on_device(queries, keys, values, out_weight, span, counts):
    per_frame, head_width = queries.shape
    frames = lax.axis_size("frame")
    groups = lax.axis_size("head")
    frame = lax.axis_index("frame").astype(jnp.int32).reshape(1)
    group = lax.axis_index("head").astype(jnp.int32).reshape(1)
    scalars = (frame, span, counts)
    swap = [(i, i ^ 1) for i in range(frames)]
    by_chip = [(i, i + 2) for i in range(frames - 2)]
    to_even = [(i, i + 1) for i in range(1, frames - 1, 2)]
    upward = [(i, (i + 1) % groups) for i in range(groups)]
    downward = [(i, (i - 1) % groups) for i in range(groups)]
    after = lax.optimization_barrier

    def send(block, route, axis="frame"):
        return lax.ppermute(block, axis, route)

    def attend(sources, sides, hop, states, name):
        both = (in_hbm(queries), q_other)
        return attention_call(
            scalars, [both[side] for side in sides], sources, sides, hop, states, name
        )

    def send_all(pieces, route):
        return [(send(k, route), send(v, route)) for k, v in pieces]

    half = per_frame // 2
    hop1 = send_all([(keys[:half], values[:half]), (keys[half:], values[half:])], by_chip)
    q_other = send(queries, swap)
    blocks = column_blocks(out_weight, groups)
    weight = lax.all_to_all(blocks, "head", split_axis=0, concat_axis=0, tiled=True)
    parts = attend([(in_hbm(keys), in_hbm(values))], (0, 1), 0, None, "attend_0")
    hop1[1], parts = after((hop1[1], parts))
    hop2 = send_all(hop1, by_chip)
    parts = attend(hop1, (0, 1), 1, parts, "attend_1")
    hop2[1], parts = after((hop2[1], parts))
    hop3 = send_all(hop2, by_chip)
    own, other = attend(hop2, (0, 1), 2, parts, "attend_2")
    hop3[1], own, other = after((hop3[1], own, other))
    hop4 = send_all(hop3, to_even)
    (other,) = attend(hop3, (1,), 3, [other], "attend_3_other")
    from_other = send(other, swap)
    (own,) = attend(hop3, (0,), 3, [own], "attend_3_own")
    attended = finish_call(scalars, in_hbm(queries), hop4, own, from_other, "finish")

    def project(base, pieces, places, dtype, name):
        return project_call(group, weight, base, pieces, places, dtype, name)

    up, down = attended, attended
    held, places, total = [attended], [(None, 0)], None
    for step in (1, 2, 3):
        up, down = send(up, upward, "head"), send(down, downward, "head")
        total = project(total, held, places, jnp.float32, f"project_{step - 1}")
        held, places = [up, down], [(None, groups - step), (None, step)]
        up, total = after((up, total))
    far = [send(up[:half], upward, "head"), send(down[half:], downward, "head")]
    total = project(total, held, places, jnp.float32, "project_3")
    return project(total, far, [(0, 4), (1, 4)], jnp.bfloat16, "project_4")


def solution(mesh):
    return jax.shard_map(
        on_device,
        mesh=mesh,
        in_specs=(
            P("frame", "head"),
            P("frame", "head"),
            P("frame", "head"),
            P("head", None),
            P(),
            P(),
        ),
        out_specs=P("frame", "head"),
        check_vma=False,
    )
```

```python
import jax
import jax.numpy as jnp
from jax import lax
from jax.experimental import pallas as pl
from jax.experimental.pallas import tpu as pltpu
from jax.sharding import PartitionSpec as P

HD = 128
WIN = 8
NEG = -1e30
EXP2_SCALE = HD ** (-0.5) * 1.4426950408889634
ROW_BLOCK = 256
SMALL_VMEM = 16 << 20
LARGE_VMEM = 24 << 20
BRIEF = pl.CostEstimate(flops=1, transcendentals=0, bytes_accessed=1)
LONG = pl.CostEstimate(flops=1 << 34, transcendentals=0, bytes_accessed=1)


def _attend(limit, q_ref, k_ref, v_ref, acc_ref, top_ref):
    slots = k_ref.shape[0]

    @pl.when(limit > 0)
    def _():
        keys = k_ref[...]
        values = jnp.concatenate([v_ref[...], jnp.ones((slots, HD), jnp.bfloat16)], axis=1)
        slot = lax.broadcasted_iota(jnp.int32, (1, slots), 1)
        hidden = jnp.where(slot < limit, 0.0, NEG)
        for start in range(0, q_ref.shape[0], ROW_BLOCK):
            rows = pl.ds(start, ROW_BLOCK)
            scores = lax.dot_general(
                q_ref[rows, :], keys, (((1,), (1,)), ((), ())), preferred_element_type=jnp.float32
            )
            scores = scores + hidden
            old_top = top_ref[0, rows, :]
            new_top = jnp.maximum(old_top, jnp.max(scores, axis=1, keepdims=True))
            wide_top = jnp.tile(new_top, (1, slots // HD))
            weights = jnp.exp2((scores - wide_top) * EXP2_SCALE).astype(jnp.bfloat16)
            rescale = jnp.exp2((old_top - new_top) * EXP2_SCALE)
            acc_ref[0, rows, :] = acc_ref[0, rows, :] * jnp.tile(rescale, (1, 2)) + jnp.dot(
                weights, values, preferred_element_type=jnp.float32
            )
            top_ref[0, rows, :] = new_top


def _visible(frame, side, behind, span_ref, counts_ref):
    query = frame if side == 0 else frame + 1 - 2 * (frame % 2)
    source = frame - behind
    back = query - source
    seen = (source >= 0) & (back >= 0) & (back < span_ref[query])
    return jnp.where(seen, counts_ref[jnp.maximum(source, 0)], 0)


def _unpack(packed, acc, top):
    acc[0, :, :HD] = packed[0, :, :HD]
    acc[0, :, HD:] = jnp.broadcast_to(packed[0, :, 2 * HD - 1 :], (acc.shape[1], HD))
    top[0] = jnp.broadcast_to(packed[0, :, HD : HD + 1], (acc.shape[1], HD))


def _join(packed, acc, top):
    new_top = jnp.maximum(top[0], packed[0, :, HD : HD + 1])
    own_part = jnp.exp2((top[0] - new_top) * EXP2_SCALE)
    other_part = jnp.exp2((packed[0, :, HD : HD + 1] - new_top) * EXP2_SCALE)
    acc[0, :, :HD] = acc[0, :, :HD] * own_part + packed[0, :, :HD] * other_part
    acc[0, :, HD:] = acc[0, :, HD:] * own_part + packed[0, :, 2 * HD - 1 :] * other_part
    top[0] = new_top


def _attention_body(sides, hops, first):
    def body(frame_ref, span_ref, counts_ref, *refs):
        refs = list(refs)
        take = lambda n: [refs.pop(0) for _ in range(n)]
        q_refs = take(len(sides))
        kv_refs = [take(2) for _ in hops]
        state_refs = [None] * len(sides) if first else take(len(sides))
        out_refs = take(len(sides))
        scratch = [take(2) for _ in sides]
        frame = frame_ref[0]
        for state, (acc, top) in zip(state_refs, scratch):
            if first:
                acc[...] = jnp.zeros_like(acc)
                top[...] = jnp.full_like(top, NEG)
            else:
                _unpack(state, acc, top)
        for hop, (k_ref, v_ref) in zip(hops, kv_refs):
            for side, q_ref, (acc, top) in zip(sides, q_refs, scratch):
                limit = _visible(frame, side, 2 * hop, span_ref, counts_ref)
                _attend(limit, q_ref, k_ref, v_ref, acc, top)
        lane = lax.broadcasted_iota(jnp.int32, (1, HD), 1)
        for out, (acc, top) in zip(out_refs, scratch):
            out[0, :, :HD] = acc[0, :, :HD]
            out[0, :, HD:] = jnp.where(lane < HD // 2, top[0], acc[0, :, HD:])

    return body


def _specs(per_frame):
    column = pl.BlockSpec((per_frame, HD), lambda h, *_: (0, h))
    packed = pl.BlockSpec((1, per_frame, 2 * HD), lambda h, *_: (h, 0, 0))
    scratch = [pltpu.VMEM((1, per_frame, 2 * HD), jnp.float32), pltpu.VMEM((1, per_frame, HD), jnp.float32)]
    return column, packed, scratch


def attention_call(scalars, queries, sources, sides, hops, states, name):
    per_frame, width = queries[0].shape
    heads = width // HD
    column, packed, scratch = _specs(per_frame)
    operands = list(queries) + [array for pair in sources for array in pair] + list(states or ())
    return pl.pallas_call(
        _attention_body(sides, hops, states is None),
        out_shape=[jax.ShapeDtypeStruct((heads, per_frame, 2 * HD), jnp.float32)] * len(sides),
        grid_spec=pltpu.PrefetchScalarGridSpec(
            num_scalar_prefetch=3,
            grid=(heads,),
            in_specs=[column] * (len(sides) + 2 * len(hops)) + [packed] * len(states or ()),
            out_specs=[packed] * len(sides),
            scratch_shapes=scratch * len(sides),
        ),
        cost_estimate=LONG,
        compiler_params=pltpu.CompilerParams(vmem_limit_bytes=SMALL_VMEM),
        name=name,
    )(*scalars, *operands)


def _finish_body(frame_ref, span_ref, counts_ref, q_ref, k_ref, v_ref, own, other, out_ref, acc, top):
    _unpack(own, acc, top)
    limit = _visible(frame_ref[0], 0, WIN - 1, span_ref, counts_ref)
    limit = jnp.where(frame_ref[0] % 2 == 0, limit, 0)
    _attend(limit, q_ref, k_ref, v_ref, acc, top)
    _join(other, acc, top)
    out_ref[...] = (acc[0, :, :HD] / acc[0, :, HD:]).astype(jnp.bfloat16)


def finish_call(scalars, queries, keys, values, own, other, name):
    per_frame, width = queries.shape
    column, packed, scratch = _specs(per_frame)
    return pl.pallas_call(
        _finish_body,
        out_shape=jax.ShapeDtypeStruct((per_frame, width), jnp.bfloat16),
        grid_spec=pltpu.PrefetchScalarGridSpec(
            num_scalar_prefetch=3,
            grid=(width // HD,),
            in_specs=[column, column, column, packed, packed],
            out_specs=column,
            scratch_shapes=scratch,
        ),
        cost_estimate=BRIEF,
        compiler_params=pltpu.CompilerParams(vmem_limit_bytes=SMALL_VMEM),
        name=name,
    )(*scalars, queries, keys, values, own, other)


def in_hbm(array):
    return pltpu.with_memory_space_constraint(array, pltpu.HBM)


def _column_blocks_body(w_ref, out_ref):
    groups, _, columns = out_ref.shape
    for group in range(groups):
        out_ref[group] = w_ref[:, group * columns : (group + 1) * columns]


def column_blocks(weight, groups):
    rows, width = weight.shape
    columns = width // groups
    return pl.pallas_call(
        _column_blocks_body,
        out_shape=pltpu.HBM((groups, rows, columns), weight.dtype),
        grid=(2,),
        in_specs=[pl.BlockSpec((rows // 2, width), lambda r: (r, 0))],
        out_specs=pl.BlockSpec((groups, rows // 2, columns), lambda r: (0, r, 0)),
        cost_estimate=BRIEF,
        compiler_params=pltpu.CompilerParams(vmem_limit_bytes=SMALL_VMEM),
        name="column_blocks",
    )(in_hbm(weight))


def _project_body(places, has_base):
    def body(group_ref, *refs):
        out_ref, w_ref = refs[-1], refs[-2]
        groups, half = w_ref.shape[0], out_ref.shape[0] // 2
        for part in (0, 1):
            rows = pl.ds(part * half, half)
            total = refs[0][rows, :] if has_base else jnp.zeros((half, out_ref.shape[1]), jnp.float32)
            for (place, offset), ref in zip(places, refs[has_base:-2], strict=True):
                if place in (part, None):
                    source = lax.rem(group_ref[0] + offset, groups)
                    piece = ref[rows, :] if place is None else ref[...]
                    total += jnp.dot(piece, w_ref[source], preferred_element_type=jnp.float32)
            out_ref[rows, :] = total.astype(out_ref.dtype)

    return body


def project_call(group, weight, base, pieces, places, dtype, name):
    groups, _, columns = weight.shape
    per_frame = pieces[0].shape[0] * (1 if places[0][0] is None else 2)
    operands = ([] if base is None else [base]) + list(pieces) + [weight]
    return pl.pallas_call(
        _project_body(places, base is not None),
        out_shape=jax.ShapeDtypeStruct((per_frame, columns), dtype),
        grid_spec=pltpu.PrefetchScalarGridSpec(
            num_scalar_prefetch=1,
            grid=(1,),
            in_specs=[pl.BlockSpec(x.shape, lambda i, g, n=x.ndim: (0,) * n) for x in operands],
            out_specs=pl.BlockSpec((per_frame, columns), lambda i, g: (0, 0)),
        ),
        cost_estimate=LONG,
        compiler_params=pltpu.CompilerParams(vmem_limit_bytes=LARGE_VMEM),
        name=name,
    )(group, *operands)


def on_device(queries, keys, values, out_weight, span, counts):
    per_frame, head_width = queries.shape
    frames = lax.axis_size("frame")
    groups = lax.axis_size("head")
    frame = lax.axis_index("frame").astype(jnp.int32).reshape(1)
    group = lax.axis_index("head").astype(jnp.int32).reshape(1)
    scalars = (frame, span, counts)
    swap = [(i, i ^ 1) for i in range(frames)]
    by_chip = [(i, i + 2) for i in range(frames - 2)]
    to_even = [(i, i + 1) for i in range(1, frames - 1, 2)]
    upward = [(i, (i + 1) % groups) for i in range(groups)]
    downward = [(i, (i - 1) % groups) for i in range(groups)]
    after = lax.optimization_barrier

    def send(block, route, axis="frame"):
        return lax.ppermute(block, axis, route)

    def attend(sources, sides, hops, states, name):
        both = (in_hbm(queries), q_other)
        return attention_call(
            scalars, [both[side] for side in sides], sources, sides, hops, states, name
        )

    k1, v1 = send(keys, by_chip), send(values, by_chip)
    q_other = send(queries, swap)
    blocks = column_blocks(out_weight, groups)
    weight = lax.all_to_all(blocks, "head", split_axis=0, concat_axis=0, tiled=True)
    parts = attend([(in_hbm(keys), in_hbm(values))], (0, 1), (0,), None, "attend_0")
    k2, v2 = send(k1, by_chip), send(v1, by_chip)
    parts = attend([(k1, v1)], (0, 1), (1,), parts, "attend_1")
    k3, v3 = send(k2, by_chip), send(v2, by_chip)
    own, other = attend([(k2, v2)], (0, 1), (2,), parts, "attend_2")
    k3, v3, own, other = after((k3, v3, own, other))
    (other,) = attend([(k3, v3)], (1,), (3,), [other], "attend_3_other")
    from_other = send(other, swap)
    k4, v4 = send(k3, to_even), send(v3, to_even)
    (own,) = attend([(k3, v3)], (0,), (3,), [own], "attend_3_own")
    attended = finish_call(scalars, in_hbm(queries), k4, v4, own, from_other, "finish")

    def project(base, pieces, places, dtype, name):
        return project_call(group, weight, base, pieces, places, dtype, name)

    half = per_frame // 2
    up, down = attended, attended
    held, places, total = [attended], [(None, 0)], None
    for step in (1, 2, 3):
        up, down = send(up, upward, "head"), send(down, downward, "head")
        total = project(total, held, places, jnp.float32, f"project_{step - 1}")
        held, places = [up, down], [(None, groups - step), (None, step)]
    far = [send(up[:half], upward, "head"), send(down[half:], downward, "head")]
    total = project(total, held, places, jnp.float32, "project_3")
    return project(total, far, [(0, 4), (1, 4)], jnp.bfloat16, "project_4")


def solution(mesh):
    return jax.shard_map(
        on_device,
        mesh=mesh,
        in_specs=(
            P("frame", "head"),
            P("frame", "head"),
            P("frame", "head"),
            P("head", None),
            P(),
            P(),
        ),
        out_specs=P("frame", "head"),
        check_vma=False,
    )
```

```python
import jax
import jax.numpy as jnp
from jax import lax
from jax.experimental import pallas as pl
from jax.experimental.pallas import tpu as pltpu
from jax.sharding import PartitionSpec as P

HD = 128
WIN = 8
NEG = -1e30
EXP2_SCALE = HD ** (-0.5) * 1.4426950408889634
ROW_BLOCK = 256
SMALL_VMEM = 16 << 20
LARGE_VMEM = 24 << 20
BRIEF = pl.CostEstimate(flops=1, transcendentals=0, bytes_accessed=1)
LONG = pl.CostEstimate(flops=1 << 34, transcendentals=0, bytes_accessed=1)


def _attend(limit, q_ref, k_ref, v_ref, acc_ref, top_ref):
    slots = k_ref.shape[0]

    @pl.when(limit > 0)
    def _():
        keys = k_ref[...]
        values = jnp.concatenate([v_ref[...], jnp.ones((slots, HD), jnp.bfloat16)], axis=1)
        slot = lax.broadcasted_iota(jnp.int32, (1, slots), 1)
        hidden = jnp.where(slot < limit, 0.0, NEG)
        for start in range(0, q_ref.shape[0], ROW_BLOCK):
            rows = pl.ds(start, ROW_BLOCK)
            scores = lax.dot_general(
                q_ref[rows, :], keys, (((1,), (1,)), ((), ())), preferred_element_type=jnp.float32
            )
            scores = scores + hidden
            old_top = top_ref[0, rows, :]
            new_top = jnp.maximum(old_top, jnp.max(scores, axis=1, keepdims=True))
            wide_top = jnp.tile(new_top, (1, slots // HD))
            weights = jnp.exp2((scores - wide_top) * EXP2_SCALE).astype(jnp.bfloat16)
            rescale = jnp.exp2((old_top - new_top) * EXP2_SCALE)
            acc_ref[0, rows, :] = acc_ref[0, rows, :] * jnp.tile(rescale, (1, 2)) + jnp.dot(
                weights, values, preferred_element_type=jnp.float32
            )
            top_ref[0, rows, :] = new_top


def _visible(frame, side, behind, span_ref, counts_ref):
    query = frame if side == 0 else frame + 1 - 2 * (frame % 2)
    source = frame - behind
    back = query - source
    seen = (source >= 0) & (back >= 0) & (back < span_ref[query])
    return jnp.where(seen, counts_ref[jnp.maximum(source, 0)], 0)


def _unpack(packed, acc, top):
    acc[0, :, :HD] = packed[0, :, :HD]
    acc[0, :, HD:] = jnp.broadcast_to(packed[0, :, 2 * HD - 1 :], (acc.shape[1], HD))
    top[0] = jnp.broadcast_to(packed[0, :, HD : HD + 1], (acc.shape[1], HD))


def _attention_body(sides, hops, first):
    def body(frame_ref, span_ref, counts_ref, *refs):
        refs = list(refs)
        take = lambda n: [refs.pop(0) for _ in range(n)]
        q_refs = take(len(sides))
        kv_refs = [take(2) for _ in hops]
        state_refs = [None] * len(sides) if first else take(len(sides))
        out_refs = take(len(sides))
        scratch = [take(2) for _ in sides]
        frame = frame_ref[0]
        for state, (acc, top) in zip(state_refs, scratch):
            if first:
                acc[...] = jnp.zeros_like(acc)
                top[...] = jnp.full_like(top, NEG)
            else:
                _unpack(state, acc, top)
        for hop, (k_ref, v_ref) in zip(hops, kv_refs):
            for side, q_ref, (acc, top) in zip(sides, q_refs, scratch):
                limit = _visible(frame, side, 2 * hop, span_ref, counts_ref)
                _attend(limit, q_ref, k_ref, v_ref, acc, top)
        lane = lax.broadcasted_iota(jnp.int32, (1, HD), 1)
        for out, (acc, top) in zip(out_refs, scratch):
            out[0, :, :HD] = acc[0, :, :HD]
            out[0, :, HD:] = jnp.where(lane < HD // 2, top[0], acc[0, :, HD:])

    return body


def _specs(per_frame):
    column = pl.BlockSpec((per_frame, HD), lambda h, *_: (0, h))
    packed = pl.BlockSpec((1, per_frame, 2 * HD), lambda h, *_: (h, 0, 0))
    scratch = [pltpu.VMEM((1, per_frame, 2 * HD), jnp.float32), pltpu.VMEM((1, per_frame, HD), jnp.float32)]
    return column, packed, scratch


def attention_call(scalars, queries, sources, sides, hops, states, name, cost):
    per_frame, width = queries[0].shape
    heads = width // HD
    column, packed, scratch = _specs(per_frame)
    operands = list(queries) + [array for pair in sources for array in pair] + list(states or ())
    return pl.pallas_call(
        _attention_body(sides, hops, states is None),
        out_shape=[jax.ShapeDtypeStruct((heads, per_frame, 2 * HD), jnp.float32)] * len(sides),
        grid_spec=pltpu.PrefetchScalarGridSpec(
            num_scalar_prefetch=3,
            grid=(heads,),
            in_specs=[column] * (len(sides) + 2 * len(hops)) + [packed] * len(states or ()),
            out_specs=[packed] * len(sides),
            scratch_shapes=scratch * len(sides),
        ),
        cost_estimate=cost,
        compiler_params=pltpu.CompilerParams(vmem_limit_bytes=SMALL_VMEM),
        name=name,
    )(*scalars, *operands)


def _join(packed, acc, top):
    new_top = jnp.maximum(top[0], packed[0, :, HD : HD + 1])
    own_part = jnp.exp2((top[0] - new_top) * EXP2_SCALE)
    other_part = jnp.exp2((packed[0, :, HD : HD + 1] - new_top) * EXP2_SCALE)
    acc[0, :, :HD] = acc[0, :, :HD] * own_part + packed[0, :, :HD] * other_part
    acc[0, :, HD:] = acc[0, :, HD:] * own_part + packed[0, :, 2 * HD - 1 :] * other_part
    top[0] = new_top


def _finish_body(frame_ref, span_ref, counts_ref, q_ref, k_ref, v_ref, own, other, upper_ref, lower_ref, acc, top):
    _unpack(own, acc, top)
    limit = _visible(frame_ref[0], 0, WIN - 1, span_ref, counts_ref)
    limit = jnp.where(frame_ref[0] % 2 == 0, limit, 0)
    _attend(limit, q_ref, k_ref, v_ref, acc, top)
    _join(other, acc, top)
    mixed = (acc[0, :, :HD] / acc[0, :, HD:]).astype(jnp.bfloat16)
    half = upper_ref.shape[0]
    upper_ref[...] = mixed[:half]
    lower_ref[...] = mixed[half:]


def finish_call(scalars, queries, keys, values, own, other, name):
    per_frame, width = queries.shape
    column, packed, scratch = _specs(per_frame)
    return pl.pallas_call(
        _finish_body,
        out_shape=[jax.ShapeDtypeStruct((per_frame // 2, width), jnp.bfloat16)] * 2,
        grid_spec=pltpu.PrefetchScalarGridSpec(
            num_scalar_prefetch=3,
            grid=(width // HD,),
            in_specs=[column, column, column, packed, packed],
            out_specs=[pl.BlockSpec((per_frame // 2, HD), lambda h, *_: (0, h))] * 2,
            scratch_shapes=scratch,
        ),
        cost_estimate=BRIEF,
        compiler_params=pltpu.CompilerParams(vmem_limit_bytes=SMALL_VMEM),
        name=name,
    )(*scalars, queries, keys, values, own, other)


def in_hbm(array):
    return pltpu.with_memory_space_constraint(array, pltpu.HBM)


def _column_blocks_body(w_ref, out_ref):
    groups, _, columns = out_ref.shape
    for group in range(groups):
        out_ref[group] = w_ref[:, group * columns : (group + 1) * columns]


def column_blocks(weight, groups):
    rows, width = weight.shape
    columns = width // groups
    return pl.pallas_call(
        _column_blocks_body,
        out_shape=pltpu.HBM((groups, rows, columns), weight.dtype),
        grid=(2,),
        in_specs=[pl.BlockSpec((rows // 2, width), lambda r: (r, 0))],
        out_specs=pl.BlockSpec((groups, rows // 2, columns), lambda r: (0, r, 0)),
        cost_estimate=BRIEF,
        compiler_params=pltpu.CompilerParams(vmem_limit_bytes=SMALL_VMEM),
        name="column_blocks",
    )(in_hbm(weight))


def _project_body(places, has_base):
    def body(group_ref, *refs):
        out_ref, w_ref = refs[-1], refs[-2]
        groups, half = w_ref.shape[0], out_ref.shape[0] // 2
        for part in (0, 1):
            rows = pl.ds(part * half, half)
            total = refs[0][rows, :] if has_base else None
            for (place, offset), ref in zip(places, refs[has_base:-2], strict=True):
                if place == part:
                    source = lax.rem(group_ref[0] + offset, groups)
                    product = jnp.dot(ref[...], w_ref[source], preferred_element_type=jnp.float32)
                    total = product if total is None else total + product
            out_ref[rows, :] = total.astype(out_ref.dtype)

    return body


def project_call(group, weight, base, pieces, places, dtype, name):
    groups, height, columns = weight.shape
    half = pieces[0].shape[0]
    operands = ([] if base is None else [base]) + list(pieces) + [weight]
    return pl.pallas_call(
        _project_body(places, base is not None),
        out_shape=jax.ShapeDtypeStruct((2 * half, columns), dtype),
        grid_spec=pltpu.PrefetchScalarGridSpec(
            num_scalar_prefetch=1,
            grid=(1,),
            in_specs=[pl.BlockSpec(x.shape, lambda i, g, n=x.ndim: (0,) * n) for x in operands],
            out_specs=pl.BlockSpec((2 * half, columns), lambda i, g: (0, 0)),
        ),
        cost_estimate=LONG,
        compiler_params=pltpu.CompilerParams(vmem_limit_bytes=LARGE_VMEM),
        name=name,
    )(group, *operands)


def on_device(queries, keys, values, out_weight, span, counts):
    per_frame, head_width = queries.shape
    frames = lax.axis_size("frame")
    groups = lax.axis_size("head")
    frame = lax.axis_index("frame").astype(jnp.int32).reshape(1)
    group = lax.axis_index("head").astype(jnp.int32).reshape(1)
    scalars = (frame, span, counts)
    swap = [(i, i ^ 1) for i in range(frames)]
    by_chip = [(i, i + 2) for i in range(frames - 2)]
    to_even = [(i, i + 1) for i in range(1, frames - 1, 2)]
    upward = [(i, (i + 1) % groups) for i in range(groups)]
    downward = [(i, (i - 1) % groups) for i in range(groups)]
    after = lax.optimization_barrier

    def send(block, route, axis="frame"):
        return lax.ppermute(block, axis, route)

    def attend(sources, sides, hops, states, name, cost=BRIEF):
        both = (in_hbm(queries), q_other)
        return attention_call(
            scalars, [both[side] for side in sides], sources, sides, hops, states, name, cost
        )

    k1, v1 = send(keys, by_chip), send(values, by_chip)
    q_other = send(queries, swap)
    k2, v2 = send(k1, by_chip), send(v1, by_chip)
    near = [(in_hbm(keys), in_hbm(values)), (k1, v1)]
    own, other = attend(near, (0, 1), (0, 1), None, "attend_01", LONG)
    blocks = column_blocks(out_weight, groups)
    weight = lax.all_to_all(blocks, "head", split_axis=0, concat_axis=0, tiled=True)
    k3, v3 = send(k2, by_chip), send(v2, by_chip)
    own, other = attend([(k2, v2)], (0, 1), (2,), [own, other], "attend_2", LONG)
    k3, v3, own, other = after((k3, v3, own, other))
    (other,) = attend([(k3, v3)], (1,), (3,), [other], "attend_3_other")
    from_other = send(other, swap)
    k4, v4 = send(k3, to_even), send(v3, to_even)
    (own,) = attend([(k3, v3)], (0,), (3,), [own], "attend_3_own", LONG)
    attended = finish_call(scalars, in_hbm(queries), k4, v4, own, from_other, "finish")

    def project(base, pieces, places, dtype, name):
        return project_call(group, weight, base, pieces, places, dtype, name)

    up, down = list(attended), list(attended)
    held, places, total = list(attended), ((0, 0), (1, 0)), None
    for step in (1, 2, 3):
        up = [send(block, upward, "head") for block in up]
        down = [send(block, downward, "head") for block in down]
        total = project(total, held, places, jnp.float32, f"project_{step - 1}")
        held = up + down
        places = ((0, groups - step), (1, groups - step), (0, step), (1, step))
    far = [send(up[0], upward, "head"), send(down[1], downward, "head")]
    total = project(total, held, places, jnp.float32, "project_3")
    return project(total, far, ((0, 4), (1, 4)), jnp.bfloat16, "project_4")


def solution(mesh):
    return jax.shard_map(
        on_device,
        mesh=mesh,
        in_specs=(
            P("frame", "head"),
            P("frame", "head"),
            P("frame", "head"),
            P("head", None),
            P(),
            P(),
        ),
        out_specs=P("frame", "head"),
        check_vma=False,
    )
```
